32 devices in a mesh: dp: 16 (over z, y, core), fsdp: 2 (over x).
Axes of the slice: x: 2, y: 2, z: 4, core: 2. Of those that a mesh axis runs over, the one named last changes fastest.
Arguments:
- hidden_in: bfloat16 [4096, 1024], P(('dp', 'fsdp')), may hold values from -6 to 6
- doc_id: int32 [4096], P(('dp', 'fsdp')), may hold values from 0 to 128, as said below
- expert_ids: int32 [4096, 8], P(('dp', 'fsdp')), may hold values from 0 to 15, all different within a row
- out_grad: bfloat16 [4096, 1024], P(('dp', 'fsdp')), may hold values from -6 to 6
- attn_gain: bfloat16 [1024], P(('dp', 'fsdp')), may hold values from 0.5 to 1.5
- query_weight: bfloat16 [1024, 1024], P(('dp', 'fsdp')), may hold values from -0.1875 to 0.1875
- key_weight: bfloat16 [1024, 512], P(('dp', 'fsdp')), may hold values from -0.1875 to 0.1875
- value_weight: bfloat16 [1024, 512], P(('dp', 'fsdp')), may hold values from -0.1875 to 0.1875
- output_weight: bfloat16 [1024, 1024], P(('dp', 'fsdp')), may hold values from -0.75 to 0.75
- ffn_gain: bfloat16 [1024], P(('dp', 'fsdp')), may hold values from 0.5 to 1.5
- router_weight: bfloat16 [1024, 16], P(('dp', 'fsdp')), may hold values from -0.375 to 0.375
- expert_gate: bfloat16 [16, 1024, 512], P('dp', 'fsdp'), may hold values from -0.1875 to 0.1875
- expert_up: bfloat16 [16, 1024, 512], P('dp', 'fsdp'), may hold values from -0.1875 to 0.1875
- expert_down: bfloat16 [16, 512, 1024], P('dp', 'fsdp'), may hold values from -1 to 1
Outputs:
- layer_out: bfloat16 [4096, 1024], P(('dp', 'fsdp'))
- grad_in: bfloat16 [4096, 1024], P(('dp', 'fsdp'))
- grad_attn_gain: float32 [1024], P(('dp', 'fsdp'))
- grad_query: float32 [1024, 1024], P(('dp', 'fsdp'))
- grad_key: float32 [1024, 512], P(('dp', 'fsdp'))
- grad_value: float32 [1024, 512], P(('dp', 'fsdp'))
- grad_output: float32 [1024, 1024], P(('dp', 'fsdp'))
- grad_ffn_gain: float32 [1024], P(('dp', 'fsdp'))
- grad_router: float32 [1024, 16], P(('dp', 'fsdp'))
- grad_expert_gate: float32 [16, 1024, 512], P('dp', 'fsdp')
- grad_expert_up: float32 [16, 1024, 512], P('dp', 'fsdp')
- grad_expert_down: float32 [16, 512, 1024], P('dp', 'fsdp')
The draws below stay inside these ranges and needn't reach their ends.
Inputs may be any that keep to these rules, and one draw needn't show every extreme that they name: Within each block of 128 rows doc_id starts at 0 and never falls; live rows come first and carry ids below 128; the rows after them carry 128 (padding). Every block has 64 or more live rows and some block has no padding. `expert_ids`: each row names 8 different experts.
All inputs are finite; a program needn't handle non-finite values.
Results may differ from the reference program's by a relative error of at most 0.015.
The reference program's roundings to bfloat16 on the way count: a program that leaves them out, or rounds other values in their place, can miss the bound.
Values may be sent and summed in bfloat16 or wider, within the bound.
A program may use at most 128 MiB of HBM per device.

```python
import jax
import jax.numpy as jnp
from jax import lax

D = 1024
HEADS = 16
KV_HEADS = 8
HEAD_DIM = 64
FF = 512
TOP = 8
TOK_DEV = 128
EXPERTS = 16
CAP = 24
TOKENS = 4096


def draw_doc_id(key, part):
    blocks = TOKENS // TOK_DEV
    key_live, key_full, key_cuts = jax.random.split(jax.random.fold_in(key, 17), 3)
    live_count = jax.random.randint(key_live, (blocks,), TOK_DEV // 2, TOK_DEV + 1)
    fullest = jax.random.randint(key_full, (), 0, blocks)
    live_count = jnp.where(jnp.arange(blocks) == fullest, TOK_DEV, live_count)
    cuts = jax.random.randint(key_cuts, (blocks, TOK_DEV), 0, 32)
    position = jnp.arange(TOK_DEV)
    starts = jnp.where(position[None, :] == 0, 1, (cuts == 0).astype(jnp.int32))
    numbers = jnp.cumsum(starts, axis=1) - 1
    numbers = jnp.where(position[None, :] < live_count[:, None], numbers, TOK_DEV)
    return numbers.reshape(TOKENS).astype(jnp.int32)


def shard_levels(key, shape, pieces, low, high):
    def one(dim, blocks):
        steps = jax.random.uniform(jax.random.fold_in(jax.random.fold_in(key, 6), dim), (blocks,), jnp.float32, low / len(pieces), high / len(pieces))
        return jnp.repeat(jnp.exp(steps), shape[dim] // blocks).reshape((-1,) + (1,) * (len(shape) - dim - 1))

    loudness = one(*pieces[0])
    for cut in pieces[1:]:
        loudness = loudness * one(*cut)
    return loudness


def choose_distinct(rng, rows, amount, top, lift):
    sequence = jax.random.permutation(jax.random.fold_in(rng, 1), amount)
    boost = sequence
    for power in range(3):
        boost = boost * boost // amount
    boost = boost * lift // amount
    tickets = jax.random.randint(jax.random.fold_in(rng, 2), (rows, amount), 0, 4096) + boost
    fixed_rows = jax.random.permutation(jax.random.fold_in(rng, 3), rows)[jnp.arange(amount) % rows]
    tickets = jnp.where(jnp.arange(rows)[:, None] == fixed_rows[None, :], 1 << 14, tickets)
    priority = tickets * amount + jnp.arange(amount)
    return lax.top_k(priority.astype(jnp.int32), top)[1].astype(jnp.int32)


def scatter_about(key, dims, scale, most, pieces=(), held_as=jnp.bfloat16):
    factor_of = shard_levels(key, dims, pieces, -0.22, 0.18) if pieces else 1.0
    drawn = jax.random.normal(key, dims, jnp.float32) * scale * factor_of
    return jnp.minimum(jnp.maximum(drawn, -most), most).astype(held_as)


def setup_inputs(seed: int = 0) -> dict:
    keys = jax.random.split(jax.random.key(seed), 15)
    hidden_in = scatter_about(keys[0], (TOKENS, D), 1.0, 6.0, ((0, 32),))
    doc_id = draw_doc_id(jax.random.fold_in(keys[14], 71), 0)
    expert_ids = choose_distinct(keys[2], TOKENS, EXPERTS, TOP, 4096)
    out_grad = scatter_about(keys[3], (TOKENS, D), 1.0, 6.0, ((0, 32),))
    attn_gain = jnp.clip(1.0 + 0.1 * jax.random.normal(keys[4], (D,), jnp.float32), 0.5, 1.5).astype(jnp.bfloat16)
    query_weight = scatter_about(keys[5], (D, HEADS * HEAD_DIM), D ** -0.5, 0.1875, ((0, 32),))
    key_weight = scatter_about(keys[6], (D, KV_HEADS * HEAD_DIM), D ** -0.5, 0.1875, ((0, 32),))
    value_weight = scatter_about(keys[7], (D, KV_HEADS * HEAD_DIM), D ** -0.5, 0.1875, ((0, 32),))
    output_weight = scatter_about(keys[8], (HEADS * HEAD_DIM, D), (D // 16) ** -0.5, 0.75, ((0, 32),))
    ffn_gain = jnp.clip(1.0 + 0.1 * jax.random.normal(keys[9], (D,), jnp.float32), 0.5, 1.5).astype(jnp.bfloat16)
    router_weight = scatter_about(keys[10], (D, EXPERTS), (D // 4) ** -0.5, 0.375, ((0, 32),))
    expert_gate = scatter_about(keys[11], (EXPERTS, D, FF), D ** -0.5, 0.1875, ((0, 16), (1, 2)))
    expert_up = scatter_about(keys[12], (EXPERTS, D, FF), D ** -0.5, 0.1875, ((0, 16), (1, 2)))
    expert_down = scatter_about(keys[13], (EXPERTS, FF, D), (FF // 16) ** -0.5, 1.0, ((0, 16), (1, 2)))
    return {"hidden_in": hidden_in, "doc_id": doc_id, "expert_ids": expert_ids, "out_grad": out_grad, "attn_gain": attn_gain, "query_weight": query_weight, "key_weight": key_weight, "value_weight": value_weight, "output_weight": output_weight, "ffn_gain": ffn_gain, "router_weight": router_weight, "expert_gate": expert_gate, "expert_up": expert_up, "expert_down": expert_down}


norm_eps = 1e-05

def round_half(values):
    return lax.optimization_barrier(values.astype(jnp.bfloat16))

def widen(values):
    return values.astype(jnp.float32)

def positions_mask(doc_block):
    row_count = doc_block.shape[0]
    row_index = jnp.arange(row_count)
    same_doc = doc_block[:, None] == doc_block[None, :]
    earlier = row_index[None, :] < row_index[:, None]
    position = lax.optimization_barrier(jnp.sum((same_doc & earlier).astype(jnp.float32), axis=1))
    allowed = same_doc & (row_index[None, :] <= row_index[:, None])
    live_rows = (doc_block < row_count).astype(jnp.float32)
    return (position, allowed, live_rows)

def rope_tables(position):
    half_dim = HEAD_DIM // 2
    freqs = jnp.exp(-jnp.log(10000.0) * (2.0 * jnp.arange(half_dim, dtype=jnp.float32) / HEAD_DIM))
    angle = position[:, None] * freqs[None, :]
    return (jnp.cos(angle), jnp.sin(angle))

def rotate(values, cosine, sinusoid):
    half_dim = values.shape[-1] // 2
    first_half, second_half = (values[..., :half_dim], values[..., half_dim:])
    return jnp.concatenate([first_half * cosine - second_half * sinusoid, second_half * cosine + first_half * sinusoid], axis=-1)

def unrotate(values, cosine, sinusoid):
    half_dim = values.shape[-1] // 2
    first_half, second_half = (values[..., :half_dim], values[..., half_dim:])
    return jnp.concatenate([first_half * cosine + second_half * sinusoid, second_half * cosine - first_half * sinusoid], axis=-1)

def norm_forward(values, gain):
    scale_row = lax.rsqrt(lax.optimization_barrier(jnp.mean(values * values, axis=-1, keepdims=True)) + norm_eps)
    normed = values * scale_row
    return (normed, scale_row, round_half(normed * gain))

def norm_backward(upstream, normed, scale_row, gain):
    scaled = upstream * gain
    inner = lax.optimization_barrier(jnp.mean(scaled * normed, axis=-1, keepdims=True))
    return (scale_row * (scaled - normed * inner), lax.optimization_barrier(jnp.sum(upstream * normed, axis=0)))

def probabilities(query_b, key_b, allowed, log_total):
    scores = jnp.einsum('ikgd,jkd->kgij', widen(query_b), widen(key_b)) * HEAD_DIM ** (-0.5)
    raised = jnp.where(allowed[None, None], jnp.exp(scores), 0.0)
    if log_total is None:
        log_total = jnp.log(lax.optimization_barrier(jnp.sum(raised, axis=-1, keepdims=True)))
    return (jnp.where(allowed[None, None], jnp.exp(scores - log_total), 0.0), log_total)

def routing(expert_block, live_rows, logits):
    experts = logits.shape[1]
    row_count = expert_block.shape[0]
    chosen = lax.optimization_barrier(jnp.sum((expert_block[:, :, None] == jnp.arange(experts)[None, None, :]).astype(jnp.float32), axis=1))
    raised = jnp.where(chosen > 0, jnp.exp(logits), 0.0)
    gates = raised / lax.optimization_barrier(jnp.sum(raised, axis=1, keepdims=True))
    member = chosen * live_rows[:, None]
    lower = (jnp.arange(row_count)[None, :] < jnp.arange(row_count)[:, None]).astype(jnp.float32)
    rank = jnp.dot(lower, member, precision=lax.Precision.HIGHEST)
    kept = member * (rank < CAP).astype(jnp.float32)
    slot_match = (rank.T[:, None, :] == jnp.arange(CAP, dtype=jnp.float32)[None, :, None]).astype(jnp.float32)
    dispatch = kept.T[:, None, :] * slot_match
    return (gates, dispatch)

def reference(hidden_in, doc_id, expert_ids, out_grad, attn_gain, query_weight, key_weight, value_weight, output_weight, ffn_gain, router_weight, expert_gate, expert_up, expert_down):
    blocks = TOKENS // TOK_DEV
    groups = HEADS // KV_HEADS
    scale = HEAD_DIM ** (-0.5)
    gate_wide = widen(expert_gate)
    up_wide = widen(expert_up)
    down_wide = widen(expert_down)
    gain_one = widen(attn_gain)
    gain_two = widen(ffn_gain)

    def one_block(totals, inputs):
        hidden_blk, doc_blk, ids_blk, grad_blk = inputs
        rows = hidden_blk.shape[0]
        position, allowed, live_rows = positions_mask(doc_blk)
        cosine, sinusoid = rope_tables(position)
        cos_query, sin_query = (cosine[:, None, None, :], sinusoid[:, None, None, :])
        cos_key, sin_key = (cosine[:, None, :], sinusoid[:, None, :])
        resid_in = widen(hidden_blk)
        normed_one, scale_one, normed_in = norm_forward(resid_in, gain_one)
        query_raw = jnp.dot(normed_in, query_weight, preferred_element_type=jnp.float32).reshape(rows, KV_HEADS, groups, HEAD_DIM)
        key_raw = jnp.dot(normed_in, key_weight, preferred_element_type=jnp.float32).reshape(rows, KV_HEADS, HEAD_DIM)
        query_b = round_half(rotate(query_raw, cos_query, sin_query))
        key_b = round_half(rotate(key_raw, cos_key, sin_key))
        value_b = round_half(jnp.dot(normed_in, value_weight, preferred_element_type=jnp.float32).reshape(rows, KV_HEADS, HEAD_DIM))
        probs, log_total = probabilities(query_b, key_b, allowed, None)
        probs_b = round_half(probs)
        mixed = jnp.einsum('kgij,jkd->ikgd', widen(probs_b), widen(value_b))
        mixed_b = round_half((mixed * live_rows[:, None, None, None]).reshape(rows, D))
        resid_mid = resid_in + jnp.dot(mixed_b, output_weight, preferred_element_type=jnp.float32)
        normed_two, scale_two, routed_in = norm_forward(resid_mid, gain_two)
        logits = jnp.dot(routed_in, router_weight, preferred_element_type=jnp.float32)
        gates, dispatch = routing(ids_blk, live_rows, logits)
        send_rows = round_half(jnp.einsum('ecr,rd->ecd', dispatch, widen(routed_in)))
        gate_pre = jnp.einsum('ecd,edf->ecf', widen(send_rows), gate_wide)
        up_pre = jnp.einsum('ecd,edf->ecf', widen(send_rows), up_wide)
        act_rows = round_half(jax.nn.silu(gate_pre) * up_pre)
        out_rows = round_half(jnp.einsum('ecf,efd->ecd', widen(act_rows), down_wide))
        combine = dispatch * gates.T[:, None, :]
        expert_sum = jnp.einsum('ecr,ecd->rd', combine, widen(out_rows), precision=lax.Precision.HIGHEST)
        layer_out = (resid_mid + expert_sum).astype(jnp.bfloat16)
        grad_out = widen(grad_blk)
        grad_send = round_half(jnp.einsum('ecr,rd->ecd', combine, grad_out, precision=lax.Precision.HIGHEST))
        row_dots = jnp.einsum('ecd,rd->ecr', widen(out_rows), grad_out, precision=lax.Precision.HIGHEST)
        grad_gates = lax.optimization_barrier(jnp.sum(dispatch * row_dots, axis=1)).T
        grad_logits = gates * (grad_gates - lax.optimization_barrier(jnp.sum(gates * grad_gates, axis=1, keepdims=True)))
        grad_logits_b = round_half(grad_logits)
        grad_act = jnp.einsum('ecd,efd->ecf', widen(grad_send), down_wide)
        sigmoid_gate = jax.nn.sigmoid(gate_pre)
        grad_up_pre = round_half(grad_act * gate_pre * sigmoid_gate)
        grad_gate_pre = round_half(grad_act * up_pre * sigmoid_gate * (1.0 + gate_pre * (1.0 - sigmoid_gate)))
        grad_down_w = jnp.einsum('ecf,ecd->efd', widen(act_rows), widen(grad_send))
        grad_gate_w = jnp.einsum('ecd,ecf->edf', widen(send_rows), widen(grad_gate_pre))
        grad_up_w = jnp.einsum('ecd,ecf->edf', widen(send_rows), widen(grad_up_pre))
        grad_rows_in = round_half(jnp.einsum('ecf,edf->ecd', widen(grad_gate_pre), gate_wide) + jnp.einsum('ecf,edf->ecd', widen(grad_up_pre), up_wide))
        grad_routed = jnp.einsum('ecr,ecd->rd', dispatch, widen(grad_rows_in)) + jnp.dot(grad_logits_b, router_weight.T, preferred_element_type=jnp.float32)
        grad_w_router = jnp.dot(routed_in.T, grad_logits_b, preferred_element_type=jnp.float32)
        grad_norm_two, grad_gain_two = norm_backward(grad_routed, normed_two, scale_two, gain_two)
        grad_mid = grad_out + grad_norm_two
        grad_mid_b = round_half(grad_mid)
        grad_w_output = jnp.dot(mixed_b.T, grad_mid_b, preferred_element_type=jnp.float32)
        grad_mixed = round_half(jnp.dot(grad_mid_b, output_weight.T, preferred_element_type=jnp.float32).reshape(rows, KV_HEADS, groups, HEAD_DIM) * live_rows[:, None, None, None])
        probs_again, unused_total = probabilities(query_b, key_b, allowed, log_total)
        grad_probs = jnp.einsum('ikgd,jkd->kgij', widen(grad_mixed), widen(value_b))
        delta = lax.optimization_barrier(jnp.sum(probs_again * grad_probs, axis=-1, keepdims=True))
        grad_scores = round_half(probs_again * (grad_probs - delta) * scale)
        grad_query_raw = jnp.einsum('kgij,jkd->ikgd', widen(grad_scores), widen(key_b))
        grad_key_raw = jnp.einsum('kgij,ikgd->jkd', widen(grad_scores), widen(query_b))
        grad_value_raw = jnp.einsum('kgij,ikgd->jkd', widen(probs_b), widen(grad_mixed))
        grad_query_b = round_half(unrotate(grad_query_raw, cos_query, sin_query).reshape(rows, HEADS * HEAD_DIM))
        grad_key_b = round_half(unrotate(grad_key_raw, cos_key, sin_key).reshape(rows, KV_HEADS * HEAD_DIM))
        grad_value_b = round_half(grad_value_raw.reshape(rows, KV_HEADS * HEAD_DIM))
        grad_w_query = jnp.dot(normed_in.T, grad_query_b, preferred_element_type=jnp.float32)
        grad_w_key = jnp.dot(normed_in.T, grad_key_b, preferred_element_type=jnp.float32)
        grad_w_value = jnp.dot(normed_in.T, grad_value_b, preferred_element_type=jnp.float32)
        grad_normed = jnp.dot(grad_query_b, query_weight.T, preferred_element_type=jnp.float32)
        grad_normed = grad_normed + jnp.dot(grad_key_b, key_weight.T, preferred_element_type=jnp.float32)
        grad_normed = grad_normed + jnp.dot(grad_value_b, value_weight.T, preferred_element_type=jnp.float32)
        grad_norm_one, grad_gain_one = norm_backward(grad_normed, normed_one, scale_one, gain_one)
        grad_input = (grad_mid + grad_norm_one).astype(jnp.bfloat16)
        terms = (grad_gain_one, grad_w_query, grad_w_key, grad_w_value, grad_w_output, grad_gain_two, grad_w_router, grad_gate_w, grad_up_w, grad_down_w)
        new_totals = tuple((total + term for total, term in zip(totals, terms)))
        return (new_totals, (layer_out, grad_input))
    experts = router_weight.shape[1]
    zeros_init = (jnp.zeros((D,), jnp.float32), jnp.zeros((D, HEADS * HEAD_DIM), jnp.float32), jnp.zeros((D, KV_HEADS * HEAD_DIM), jnp.float32), jnp.zeros((D, KV_HEADS * HEAD_DIM), jnp.float32), jnp.zeros((HEADS * HEAD_DIM, D), jnp.float32), jnp.zeros((D,), jnp.float32), jnp.zeros((D, experts), jnp.float32), jnp.zeros((experts, D, FF), jnp.float32), jnp.zeros((experts, D, FF), jnp.float32), jnp.zeros((experts, FF, D), jnp.float32))
    inputs = (hidden_in.reshape(blocks, TOK_DEV, D), doc_id.reshape(blocks, TOK_DEV), expert_ids.reshape(blocks, TOK_DEV, TOP), out_grad.reshape(blocks, TOK_DEV, D))
    totals, (layer_out, grad_input) = lax.scan(one_block, zeros_init, inputs)
    return (layer_out.reshape(TOKENS, D), grad_input.reshape(TOKENS, D), totals[0], totals[1], totals[2], totals[3], totals[4], totals[5], totals[6], totals[7], totals[8], totals[9])
```

```python
import functools

import jax
import jax.numpy as jnp
from jax import lax
from jax.experimental import pallas as pl
from jax.experimental.pallas import tpu as pltpu
from jax.sharding import PartitionSpec as P

HEADS = 16
KV_HEADS = 8
HEAD_DIM = 64
TOP = 8
CAP = 24


norm_eps = 1e-05


def positions_mask(doc_block):
    row_count = doc_block.shape[0]
    row_index = jnp.arange(row_count)
    same_doc = doc_block[:, None] == doc_block[None, :]
    earlier = row_index[None, :] < row_index[:, None]
    position = jnp.sum((same_doc & earlier).astype(jnp.float32), axis=1)
    allowed = same_doc & (row_index[None, :] <= row_index[:, None])
    live_rows = (doc_block < row_count).astype(jnp.float32)
    return (position, allowed, live_rows)


def rope_tables(position):
    half_dim = HEAD_DIM // 2
    freqs = jnp.exp(-jnp.log(10000.0) * (2.0 * jnp.arange(half_dim, dtype=jnp.float32) / HEAD_DIM))
    angle = position[:, None] * freqs[None, :]
    return (jnp.cos(angle), jnp.sin(angle))


def rotate(values, cosine, sinusoid):
    half_dim = values.shape[-1] // 2
    first_half, second_half = (values[..., :half_dim], values[..., half_dim:])
    return jnp.concatenate(
        [
            first_half * cosine - second_half * sinusoid,
            second_half * cosine + first_half * sinusoid,
        ],
        axis=-1,
    )


def unrotate(values, cosine, sinusoid):
    half_dim = values.shape[-1] // 2
    first_half, second_half = (values[..., :half_dim], values[..., half_dim:])
    return jnp.concatenate(
        [
            first_half * cosine + second_half * sinusoid,
            second_half * cosine - first_half * sinusoid,
        ],
        axis=-1,
    )


def norm_forward(values, gain):
    scale_row = lax.rsqrt(jnp.mean(values * values, axis=-1, keepdims=True) + norm_eps)
    normed = values * scale_row
    return (normed, scale_row, (normed * gain).astype(jnp.bfloat16))


def norm_backward(upstream, normed, scale_row, gain):
    scaled = upstream * gain
    inner = jnp.mean(scaled * normed, axis=-1, keepdims=True)
    return (scale_row * (scaled - normed * inner), jnp.sum(upstream * normed, axis=0))


def probabilities(query_b, key_b, allowed, log_total):
    scores = jnp.einsum(
        "ikgd,jkd->kgij", query_b, key_b, preferred_element_type=jnp.float32
    ) * HEAD_DIM ** (-0.5)
    raised = jnp.where(allowed[None, None], jnp.exp(scores), 0.0)
    if log_total is None:
        log_total = jnp.log(jnp.sum(raised, axis=-1, keepdims=True))
    return (jnp.where(allowed[None, None], jnp.exp(scores - log_total), 0.0), log_total)


def slots_of(expert_block, live_rows, experts):
    row_count = expert_block.shape[0]
    chosen = jnp.sum(
        (expert_block[:, :, None] == jnp.arange(experts)[None, None, :]).astype(jnp.float32), axis=1
    )
    member = chosen * live_rows[:, None]
    lower = (jnp.arange(row_count)[None, :] < jnp.arange(row_count)[:, None]).astype(jnp.bfloat16)
    rank = jnp.dot(lower, member.astype(jnp.bfloat16), preferred_element_type=jnp.float32)
    kept = member * (rank < CAP).astype(jnp.float32)
    slot_match = (rank.T[:, None, :] == jnp.arange(CAP, dtype=jnp.float32)[None, :, None]).astype(
        jnp.float32
    )
    dispatch = kept.T[:, None, :] * slot_match
    return (dispatch, kept, chosen, rank)


def split_bf16(values):
    high = values.astype(jnp.bfloat16)
    left = values - lax.reduce_precision(values, 8, 7)
    middle = left.astype(jnp.bfloat16)
    low = (left - lax.reduce_precision(left, 8, 7)).astype(jnp.bfloat16)
    return (high, middle, low)


def expert_forward(rows_in, w_gate, w_up, w_down):
    gate_pre = jnp.dot(rows_in, w_gate, preferred_element_type=jnp.float32)
    up_pre = jnp.dot(rows_in, w_up, preferred_element_type=jnp.float32)
    act_rows = (jax.nn.silu(gate_pre) * up_pre).astype(jnp.bfloat16)
    out_rows = jnp.dot(act_rows, w_down, preferred_element_type=jnp.float32).astype(jnp.bfloat16)
    return (gate_pre, up_pre, act_rows, out_rows)


def expert_backward(rows_in, gate_pre, up_pre, act_rows, grad_rows, w_gate, w_up, w_down):
    grad_act = jnp.dot(grad_rows, w_down.T, preferred_element_type=jnp.float32)
    sigmoid_gate = jax.nn.sigmoid(gate_pre)
    grad_up_pre = (grad_act * gate_pre * sigmoid_gate).astype(jnp.bfloat16)
    grad_gate_pre = (
        grad_act * up_pre * sigmoid_gate * (1.0 + gate_pre * (1.0 - sigmoid_gate))
    ).astype(jnp.bfloat16)
    grad_down_w = jnp.dot(act_rows.T, grad_rows, preferred_element_type=jnp.float32)
    grad_gate_w = jnp.dot(rows_in.T, grad_gate_pre, preferred_element_type=jnp.float32)
    grad_up_w = jnp.dot(rows_in.T, grad_up_pre, preferred_element_type=jnp.float32)
    grad_rows_in = jnp.dot(grad_gate_pre, w_gate.T, preferred_element_type=jnp.float32)
    grad_rows_in = (
        grad_rows_in + jnp.dot(grad_up_pre, w_up.T, preferred_element_type=jnp.float32)
    ).astype(jnp.bfloat16)
    return (grad_rows_in, grad_gate_w, grad_up_w, grad_down_w)


def axis_bits(size):
    return size.bit_length() - 1


def span(bits):
    masks = [0]
    for bit in bits:
        masks = masks + [mask | (1 << bit) for mask in masks]
    return masks


def dimension_bits(sizes):
    dp_bits, fsdp_bits = (axis_bits(sizes[0]), axis_bits(sizes[1]))
    x_bits = list(range(fsdp_bits))
    high = [fsdp_bits + bit for bit in range(dp_bits - 1, 0, -1)]
    return {"x": x_bits, "z": high[:-1], "y": high[-1:], "c": [fsdp_bits] if dp_bits else []}


def bit_order(sizes, letters):
    bits = dimension_bits(sizes)
    return [bit for letter in letters for bit in bits[letter]]


class Cube:
    def __init__(self, sizes):
        self.sizes = sizes
        self.dp = lax.axis_index("dp")
        self.fsdp = lax.axis_index("fsdp")
        self.me = self.dp * sizes[1] + self.fsdp
        self.fsdp_bits = axis_bits(sizes[1])
        self.bits = axis_bits(sizes[0]) + self.fsdp_bits
        self.flips = [
            (1 - 2 * ((self.me // (1 << bit)) % 2)) * (1 << bit) for bit in range(self.bits)
        ]

    def block(self, mask):
        index = self.me
        for bit, flip in enumerate(self.flips):
            if mask >> bit & 1:
                index = index + flip
        return index

    def device(self, mask):
        other = self.block(mask)
        return {"dp": other // self.sizes[1], "fsdp": other % self.sizes[1]}

    def dp_masks(self):
        masks = [part << self.fsdp_bits for part in range(1, self.sizes[0])]
        return sorted(masks, reverse=True)

    def fsdp_masks(self):
        return list(range(1, self.sizes[1]))

    def greet(self, masks):
        barrier = pltpu.get_barrier_semaphore()
        for mask in masks:
            pl.semaphore_signal(
                barrier, inc=1, device_id=self.device(mask), device_id_type=pl.DeviceIdType.MESH
            )
        pl.semaphore_wait(barrier, len(masks))

    def send(self, source, target, send_sem, recv_sem, mask):
        copy = pltpu.make_async_remote_copy(
            src_ref=source,
            dst_ref=target,
            send_sem=send_sem,
            recv_sem=recv_sem,
            device_id=self.device(mask),
            device_id_type=pl.DeviceIdType.MESH,
        )
        copy.start()
        return copy


def link_time(sizes, bit, volume):
    return volume / (8.0 if bit in dimension_bits(sizes)["c"] else 1.0)


def gather_plan(sizes, orders, volumes):
    free = {}
    known = [{0: 0.0} for _ in orders]
    waiting = []
    for which, order in enumerate(orders):
        for stage, bit in enumerate(order):
            for mask in span(order[:stage]):
                waiting.append((which, mask, bit, len(order) - stage))
    plan = []
    while waiting:
        best = None
        for item in waiting:
            which, mask, bit, left = item
            if mask not in known[which]:
                continue
            begin = max(known[which][mask], free.get(bit, 0.0))
            rank = (begin, -left, which, mask)
            if best is None or rank < best[0]:
                best = (rank, item)
        (begin, _, _, _), item = best
        which, mask, bit, _ = item
        end = begin + link_time(sizes, bit, volumes[which])
        free[bit] = end
        known[which][mask | (1 << bit)] = end + 0.3 * min(volumes)
        plan.append((which, mask, bit))
        waiting.remove(item)
    return plan


def scatter_plan(sizes, orders, volumes):
    free = {}
    known = [{} for _ in orders]
    waiting = []
    for which, order in enumerate(orders):
        for stage, bit in enumerate(order):
            for rest in span(order[stage + 1 :]):
                waiting.append((which, stage, rest | (1 << bit)))
    plan = []
    while waiting:
        best = None
        for item in waiting:
            which, stage, mask = item
            needs = [mask | (1 << earlier) for earlier in orders[which][:stage]]
            if any(need not in known[which] for need in needs):
                continue
            bit = orders[which][stage]
            ready = max([known[which][need] for need in needs], default=0.0)
            begin = max(ready, free.get(bit, 0.0))
            after = [at for at, later in enumerate(orders[which]) if mask >> later & 1 and at > stage]
            rank = (begin, after[0] if after else len(orders[which]), which, mask)
            if best is None or rank < best[0]:
                best = (rank, item)
        rank, item = best
        which, stage, mask = item
        bit = orders[which][stage]
        end = rank[0] + link_time(sizes, bit, volumes[which])
        free[bit] = end
        known[which][mask] = end + 0.3 * min(volumes)
        plan.append(item)
        waiting.remove(item)
    return plan


def volume_of(shape):
    total = 1
    for size in shape:
        total = total * size
    return total


GATHER_ORDERS = ("xzyc", "xzyc", "xzyc", "zxyc", "xzyc")
SCATTER_ORDERS = ("zyxc", "xyzc", "zyxc", "zxyc", "zxyc")


def front_kernel(sizes, count, *refs):
    shards, experts, rows = (refs[:count], refs[count : count + 3], refs[count + 3])
    outs = refs[count + 4 :]
    full, wide, rows_out = (outs[:count], outs[count : count + 3], outs[count + 3])
    local_sems, send_sems, recv_sems, wide_send, wide_recv, row_send, row_recv = outs[count + 4 :]
    cube = Cube(sizes)
    singles = [1 << bit for bit in range(cube.bits)]
    cube.greet(sorted(set(singles + cube.dp_masks() + cube.fsdp_masks())))
    own = []
    for which, (source, target) in enumerate(zip(shards, full)):
        own.append((source, target.at[cube.me]))
    for which, (source, target) in enumerate(zip(experts, wide)):
        own.append((source, target.at[cube.fsdp]))
    own.append((rows.at[cube.dp], rows_out.at[cube.dp]))
    pending = []
    for mask in cube.fsdp_masks():
        for which, (source, target) in enumerate(zip(experts, wide)):
            pending.append(
                cube.send(
                    source,
                    target.at[cube.fsdp],
                    wide_send.at[which, mask],
                    wide_recv.at[which, mask],
                    mask,
                )
            )
    orders = [bit_order(sizes, letters) for letters in GATHER_ORDERS]
    plan = gather_plan(sizes, orders, [volume_of(ref.shape) for ref in shards])
    copies = [{} for _ in shards]
    arrived = [{0} for _ in shards]
    started = False
    for which, mask, bit in plan:
        if mask and not started:
            started = True
            for peer in cube.dp_masks():
                part = peer >> cube.fsdp_bits
                pending.append(
                    cube.send(
                        rows.at[cube.block(peer) // sizes[1]],
                        rows_out.at[cube.dp],
                        row_send.at[part],
                        row_recv.at[part],
                        peer,
                    )
                )
            for at, (source, target) in enumerate(own):
                own[at] = pltpu.make_async_copy(source, target, local_sems.at[at])
                own[at].start()
        if mask not in arrived[which]:
            copies[which][mask].wait_recv()
            arrived[which].add(mask)
        label = mask | (1 << bit)
        target = full[which]
        copies[which][label] = cube.send(
            target.at[cube.block(mask)] if mask else shards[which],
            target.at[cube.block(mask)],
            send_sems.at[which, label],
            recv_sems.at[which, label],
            1 << bit,
        )
    for which, made in enumerate(copies):
        for label, copy in made.items():
            if label not in arrived[which]:
                copy.wait_recv()
    for copy in pending:
        copy.wait_recv()
    for copy in own:
        copy.wait()
    for made in copies:
        for copy in made.values():
            copy.wait_send()
    for copy in pending:
        copy.wait_send()


def front_gather(sizes, shards, experts, rows):
    blocks = sizes[0] * sizes[1]
    count = len(shards)
    out_shape = [jax.ShapeDtypeStruct((blocks,) + part.shape, part.dtype) for part in shards]
    out_shape += [jax.ShapeDtypeStruct((sizes[1],) + part.shape, part.dtype) for part in experts]
    out_shape += [jax.ShapeDtypeStruct(rows.shape, rows.dtype)]
    dma = pltpu.SemaphoreType.DMA
    return pl.pallas_call(
        lambda *refs: front_kernel(sizes, count, *refs),
        out_shape=tuple(out_shape),
        in_specs=[pl.BlockSpec(memory_space=pltpu.VMEM)] * (count + 4),
        out_specs=(pl.BlockSpec(memory_space=pl.ANY),) * (count + 4),
        scratch_shapes=[
            dma((count + 4,)),
            dma((count, blocks)),
            dma((count, blocks)),
            dma((3, sizes[1])),
            dma((3, sizes[1])),
            dma((sizes[0],)),
            dma((sizes[0],)),
        ],
        compiler_params=pltpu.CompilerParams(
            collective_id=0, has_side_effects=True, vmem_limit_bytes=24 * 1024 * 1024
        ),
        name="front_gather",
    )(*shards, *experts, rows)


def swap_kernel(sizes, count, parts, *refs):
    rows, grads = (refs[:count], refs[count : count + parts])
    outs = refs[count + parts :]
    rows_out, grads_out = (outs[:count], outs[count : count + parts])
    local_sems, row_send, row_recv, part_send, part_recv = outs[count + parts :]
    cube = Cube(sizes)
    cube.greet(cube.dp_masks() + (cube.fsdp_masks() if parts else []))
    pending = []
    for peer in cube.dp_masks():
        part = peer >> cube.fsdp_bits
        for which in range(count):
            pending.append(
                cube.send(
                    rows[which].at[cube.block(peer) // sizes[1]],
                    rows_out[which].at[cube.dp],
                    row_send.at[which, part],
                    row_recv.at[which, part],
                    peer,
                )
            )
    for mask in cube.fsdp_masks() if parts else []:
        for which in range(parts):
            pending.append(
                cube.send(
                    grads[which].at[cube.block(mask) % sizes[1]],
                    grads_out[which].at[mask - 1],
                    part_send.at[which, mask],
                    part_recv.at[which, mask],
                    mask,
                )
            )
    own = []
    for which in range(count):
        own.append(
            pltpu.make_async_copy(
                rows[which].at[cube.dp], rows_out[which].at[cube.dp], local_sems.at[which]
            )
        )
        own[-1].start()
    for copy in pending:
        copy.wait_recv()
    for copy in own:
        copy.wait()
    for copy in pending:
        copy.wait_send()


def swap_rows(sizes, rows, grads, collective_id, name):
    count, parts = (len(rows), len(grads))
    peers = max(sizes[1] - 1, 1)
    out_shape = [jax.ShapeDtypeStruct(part.shape, part.dtype) for part in rows]
    out_shape += [
        jax.ShapeDtypeStruct((peers,) + part.shape[1:], part.dtype) for part in grads
    ]
    dma = pltpu.SemaphoreType.DMA
    return pl.pallas_call(
        lambda *refs: swap_kernel(sizes, count, parts, *refs),
        out_shape=tuple(out_shape),
        in_specs=[pl.BlockSpec(memory_space=pltpu.VMEM)] * (count + parts),
        out_specs=(pl.BlockSpec(memory_space=pl.ANY),) * (count + parts),
        scratch_shapes=[
            dma((count,)),
            dma((count, sizes[0])),
            dma((count, sizes[0])),
            dma((max(parts, 1), sizes[1])),
            dma((max(parts, 1), sizes[1])),
        ],
        compiler_params=pltpu.CompilerParams(
            collective_id=collective_id,
            has_side_effects=True,
            vmem_limit_bytes=24 * 1024 * 1024,
        ),
        name=name,
    )(*rows, *grads)


def scatter_kernel(sizes, count, *refs):
    sources, outs = (refs[:count], refs[count : 2 * count])
    slots, held = (refs[2 * count : 3 * count], refs[3 * count : 4 * count])
    send_sems, recv_sems = refs[4 * count :]
    cube = Cube(sizes)
    cube.greet([1 << bit for bit in range(cube.bits)])
    orders = [bit_order(sizes, letters)[::-1] for letters in SCATTER_ORDERS]
    copies = [{} for _ in sources]
    arrived = [set() for _ in sources]
    places = [{} for _ in sources]

    def total(which, mask, stage):
        value = sources[which][cube.block(mask)].astype(jnp.float32)
        for earlier in orders[which][:stage]:
            label = mask | (1 << earlier)
            copies[which][label].wait_recv()
            value = value + slots[which][label].astype(jnp.float32)
        return value

    for which, stage, mask in scatter_plan(
        sizes, orders, [volume_of(ref.shape) for ref in outs]
    ):
        if stage == 0:
            leaving = sources[which].at[cube.block(mask)]
        else:
            slot = places[which].setdefault(mask, len(places[which]))
            held[which][slot] = total(which, mask, stage).astype(jnp.bfloat16)
            leaving = held[which].at[slot]
        copies[which][mask] = cube.send(
            leaving,
            slots[which].at[mask],
            send_sems.at[which, mask],
            recv_sems.at[which, mask],
            1 << orders[which][stage],
        )
    for which in range(count):
        outs[which][...] = total(which, 0, len(orders[which]))
    for made in copies:
        for copy in made.values():
            copy.wait_send()


def scatter_rows(sizes, packed):
    blocks = sizes[0] * sizes[1]
    count = len(packed)
    shapes = [part.shape[1:] for part in packed]
    dma = pltpu.SemaphoreType.DMA
    return pl.pallas_call(
        lambda *refs: scatter_kernel(sizes, count, *refs),
        out_shape=tuple(jax.ShapeDtypeStruct(shape, jnp.float32) for shape in shapes),
        in_specs=[pl.BlockSpec(memory_space=pltpu.VMEM)] * count,
        out_specs=(pl.BlockSpec(memory_space=pltpu.VMEM),) * count,
        scratch_shapes=[pltpu.VMEM((blocks,) + shape, jnp.bfloat16) for shape in shapes]
        + [pltpu.VMEM((blocks // 2,) + shape, jnp.bfloat16) for shape in shapes]
        + [dma((count, blocks)), dma((count, blocks))],
        compiler_params=pltpu.CompilerParams(
            collective_id=3, has_side_effects=True, vmem_limit_bytes=48 * 1024 * 1024
        ),
        name="scatter_rows",
    )(*packed)


def shards(
    sizes,
    hidden_in,
    doc_id,
    expert_ids,
    out_grad,
    attn_gain,
    query_weight,
    key_weight,
    value_weight,
    output_weight,
    ffn_gain,
    router_weight,
    expert_gate,
    expert_up,
    expert_down,
):
    rows = hidden_in.shape[0]
    groups = HEADS // KV_HEADS
    scale = HEAD_DIM ** (-0.5)
    experts_all = router_weight.shape[1]
    query_width, key_width = (query_weight.shape[1], key_weight.shape[1])
    small_width = -(-(experts_all + 2) // 128) * 128
    small = jnp.concatenate([router_weight, attn_gain[:, None], ffn_gain[:, None]], axis=1)
    small = jnp.pad(small, ((0, 0), (0, small_width - small.shape[1])))
    position, allowed, live_rows = positions_mask(doc_id)
    dispatch, kept, chosen, rank = slots_of(expert_ids, live_rows, experts_all)
    dispatch_b = dispatch.astype(jnp.bfloat16)
    pulled_b = jnp.einsum(
        "ecr,rd->ecd", dispatch_b, out_grad, preferred_element_type=jnp.float32
    ).astype(jnp.bfloat16)
    gathered = front_gather(
        sizes,
        (query_weight, key_weight, value_weight, output_weight, small),
        (expert_gate[0], expert_up[0], expert_down[0]),
        pulled_b,
    )
    w_query, w_key, w_value, w_output, full_small = [
        part.reshape(-1, part.shape[2]) for part in gathered[:5]
    ]
    w_router = full_small[:, :experts_all]
    gain_one, gain_two = (full_small[:, experts_all], full_small[:, experts_all + 1])
    w_gate, w_up, w_down = [part.reshape(-1, part.shape[2]) for part in gathered[5:8]]
    grad_recv = gathered[8]
    cosine, sinusoid = rope_tables(position)
    cos_query, sin_query = (cosine[:, None, None, :], sinusoid[:, None, None, :])
    cos_key, sin_key = (cosine[:, None, :], sinusoid[:, None, :])
    resid_in = hidden_in.astype(jnp.float32)
    normed_one, scale_one, normed_in = norm_forward(resid_in, gain_one.astype(jnp.float32))
    query_raw = jnp.dot(normed_in, w_query, preferred_element_type=jnp.float32).reshape(
        rows, KV_HEADS, groups, HEAD_DIM
    )
    key_raw = jnp.dot(normed_in, w_key, preferred_element_type=jnp.float32).reshape(
        rows, KV_HEADS, HEAD_DIM
    )
    query_b = rotate(query_raw, cos_query, sin_query).astype(jnp.bfloat16)
    key_b = rotate(key_raw, cos_key, sin_key).astype(jnp.bfloat16)
    value_b = (
        jnp.dot(normed_in, w_value, preferred_element_type=jnp.float32)
        .reshape(rows, KV_HEADS, HEAD_DIM)
        .astype(jnp.bfloat16)
    )
    probs, log_total = probabilities(query_b, key_b, allowed, None)
    probs_b = probs.astype(jnp.bfloat16)
    mixed = jnp.einsum("kgij,jkd->ikgd", probs_b, value_b, preferred_element_type=jnp.float32)
    mixed_b = (
        (mixed * live_rows[:, None, None, None])
        .reshape(rows, HEADS * HEAD_DIM)
        .astype(jnp.bfloat16)
    )
    resid_mid = resid_in + jnp.dot(mixed_b, w_output, preferred_element_type=jnp.float32)
    normed_two, scale_two, routed_in = norm_forward(resid_mid, gain_two.astype(jnp.float32))
    logits = jnp.dot(routed_in, w_router, preferred_element_type=jnp.float32)
    raised = jnp.where(chosen > 0, jnp.exp(logits), 0.0)
    gates = raised / jnp.sum(raised, axis=1, keepdims=True)
    send_rows = jnp.einsum(
        "ecr,rd->ecd", dispatch_b, routed_in, preferred_element_type=jnp.float32
    ).astype(jnp.bfloat16)
    combine = dispatch * gates.T[:, None, :]
    slot_gate = jnp.sum(combine, axis=2, keepdims=True)
    pieces = split_bf16(slot_gate)
    lanes = jnp.arange(128)[None, None, :]
    packed_gate = sum(
        jnp.where(lanes == at, piece, jnp.zeros((), jnp.bfloat16)) for at, piece in enumerate(pieces)
    )
    (recv,) = swap_rows(
        sizes, (jnp.concatenate([send_rows, packed_gate], axis=2),), (), 1, "swap_out"
    )
    flat = recv.reshape(-1, recv.shape[2])
    width = routed_in.shape[1]
    flat_in = flat[:, :width]
    flat_gate = jnp.sum(flat[:, width : width + 3].astype(jnp.float32), axis=1, keepdims=True)
    gate_pre, up_pre, act_rows, out_rows = expert_forward(flat_in, w_gate, w_up, w_down)
    flat_grad = (flat_gate * grad_recv.reshape(flat_in.shape).astype(jnp.float32)).astype(
        jnp.bfloat16
    )
    grad_rows_in, grad_gate_w, grad_up_w, grad_down_w = expert_backward(
        flat_in, gate_pre, up_pre, act_rows, flat_grad, w_gate, w_up, w_down
    )
    expert_sums = [
        part.reshape((sizes[1], -1) + part.shape[1:])
        for part in (grad_gate_w, grad_up_w, grad_down_w)
    ]
    shape_rows = send_rows.shape
    swapped = swap_rows(
        sizes,
        (out_rows.reshape(shape_rows), grad_rows_in.reshape(shape_rows)),
        [part.astype(jnp.bfloat16) for part in expert_sums],
        2,
        "swap_back",
    )
    back_rows, grad_back = swapped[:2]
    own = lax.axis_index("fsdp")
    expert_grads = [
        lax.dynamic_index_in_dim(mine, own, axis=0, keepdims=True)
        + jnp.sum(other.astype(jnp.float32), axis=0, keepdims=True)
        for mine, other in zip(expert_sums, swapped[2:])
    ]
    expert_sum = sum(
        jnp.einsum("ecr,ecd->rd", piece, back_rows, preferred_element_type=jnp.float32)
        for piece in split_bf16(combine)[:2]
    )
    layer_out = (resid_mid + expert_sum).astype(jnp.bfloat16)
    grad_out = out_grad.astype(jnp.float32)
    slot_dot = jnp.sum(back_rows.astype(jnp.float32) * pulled_b.astype(jnp.float32), axis=2)
    grad_gates = jnp.sum(dispatch * slot_dot[:, :, None], axis=1).T
    grad_logits = gates * (grad_gates - jnp.sum(gates * grad_gates, axis=1, keepdims=True))
    grad_logits_b = grad_logits.astype(jnp.bfloat16)
    grad_routed = jnp.einsum(
        "ecr,ecd->rd", dispatch_b, grad_back, preferred_element_type=jnp.float32
    )
    grad_routed = grad_routed + jnp.dot(
        grad_logits_b, w_router.T, preferred_element_type=jnp.float32
    )
    grad_w_router = jnp.dot(routed_in.T, grad_logits_b, preferred_element_type=jnp.float32)
    grad_norm_two, grad_gain_two = norm_backward(
        grad_routed, normed_two, scale_two, gain_two.astype(jnp.float32)
    )
    grad_mid = grad_out + grad_norm_two
    grad_mid_b = grad_mid.astype(jnp.bfloat16)
    grad_w_output = jnp.dot(mixed_b.T, grad_mid_b, preferred_element_type=jnp.float32)
    grad_mixed = jnp.dot(grad_mid_b, w_output.T, preferred_element_type=jnp.float32).reshape(
        rows, KV_HEADS, groups, HEAD_DIM
    )
    grad_mixed = (grad_mixed * live_rows[:, None, None, None]).astype(jnp.bfloat16)
    probs_again, unused_total = probabilities(query_b, key_b, allowed, log_total)
    grad_probs = jnp.einsum(
        "ikgd,jkd->kgij", grad_mixed, value_b, preferred_element_type=jnp.float32
    )
    delta = jnp.sum(probs_again * grad_probs, axis=-1, keepdims=True)
    grad_scores = (probs_again * (grad_probs - delta) * scale).astype(jnp.bfloat16)
    grad_query_raw = jnp.einsum(
        "kgij,jkd->ikgd", grad_scores, key_b, preferred_element_type=jnp.float32
    )
    grad_key_raw = jnp.einsum(
        "kgij,ikgd->jkd", grad_scores, query_b, preferred_element_type=jnp.float32
    )
    grad_value_raw = jnp.einsum(
        "kgij,ikgd->jkd",
        probs_again.astype(jnp.bfloat16),
        grad_mixed,
        preferred_element_type=jnp.float32,
    )
    grad_query_b = (
        unrotate(grad_query_raw, cos_query, sin_query)
        .reshape(rows, HEADS * HEAD_DIM)
        .astype(jnp.bfloat16)
    )
    grad_key_b = (
        unrotate(grad_key_raw, cos_key, sin_key)
        .reshape(rows, KV_HEADS * HEAD_DIM)
        .astype(jnp.bfloat16)
    )
    grad_value_b = grad_value_raw.reshape(rows, KV_HEADS * HEAD_DIM).astype(jnp.bfloat16)
    grad_w_query = jnp.dot(normed_in.T, grad_query_b, preferred_element_type=jnp.float32)
    grad_w_key = jnp.dot(normed_in.T, grad_key_b, preferred_element_type=jnp.float32)
    grad_w_value = jnp.dot(normed_in.T, grad_value_b, preferred_element_type=jnp.float32)
    grad_normed = jnp.dot(grad_query_b, w_query.T, preferred_element_type=jnp.float32)
    grad_normed = grad_normed + jnp.dot(grad_key_b, w_key.T, preferred_element_type=jnp.float32)
    grad_normed = grad_normed + jnp.dot(grad_value_b, w_value.T, preferred_element_type=jnp.float32)
    grad_norm_one, grad_gain_one = norm_backward(
        grad_normed, normed_one, scale_one, gain_one.astype(jnp.float32)
    )
    grad_input = (grad_mid + grad_norm_one).astype(jnp.bfloat16)
    grad_small = jnp.concatenate(
        [grad_w_router, grad_gain_one[:, None], grad_gain_two[:, None]], axis=1
    )
    grad_small = jnp.pad(grad_small, ((0, 0), (0, small_width - grad_small.shape[1])))
    blocks = sizes[0] * sizes[1]
    own_query, own_key, own_value, own_output, own_small = scatter_rows(
        sizes,
        [
            part.astype(jnp.bfloat16).reshape(blocks, -1, part.shape[1])
            for part in (grad_w_query, grad_w_key, grad_w_value, grad_w_output, grad_small)
        ],
    )
    dense_grads = (
        own_small[:, experts_all],
        own_query,
        own_key,
        own_value,
        own_output,
        own_small[:, experts_all + 1],
        own_small[:, :experts_all],
    )
    return (
        layer_out,
        grad_input,
        dense_grads[0],
        dense_grads[1],
        dense_grads[2],
        dense_grads[3],
        dense_grads[4],
        dense_grads[5],
        dense_grads[6],
        expert_grads[0],
        expert_grads[1],
        expert_grads[2],
    )


def solution(mesh):
    in_specs = (
        P(("dp", "fsdp"), None),
        P(("dp", "fsdp")),
        P(("dp", "fsdp"), None),
        P(("dp", "fsdp"), None),
        P(("dp", "fsdp")),
        P(("dp", "fsdp"), None),
        P(("dp", "fsdp"), None),
        P(("dp", "fsdp"), None),
        P(("dp", "fsdp"), None),
        P(("dp", "fsdp")),
        P(("dp", "fsdp"), None),
        P("dp", "fsdp", None),
        P("dp", "fsdp", None),
        P("dp", "fsdp", None),
    )
    out_specs = (
        P(("dp", "fsdp"), None),
        P(("dp", "fsdp"), None),
        P(("dp", "fsdp")),
        P(("dp", "fsdp"), None),
        P(("dp", "fsdp"), None),
        P(("dp", "fsdp"), None),
        P(("dp", "fsdp"), None),
        P(("dp", "fsdp")),
        P(("dp", "fsdp"), None),
        P("dp", "fsdp", None),
        P("dp", "fsdp", None),
        P("dp", "fsdp", None),
    )
    sizes = (mesh.shape["dp"], mesh.shape["fsdp"])
    body = functools.partial(shards, sizes)
    return jax.shard_map(body, mesh=mesh, in_specs=in_specs, out_specs=out_specs, check_vma=False)
```

```python
import functools

import jax
import jax.numpy as jnp
from jax import lax
from jax.experimental import pallas as pl
from jax.experimental.pallas import tpu as pltpu
from jax.sharding import PartitionSpec as P

HEADS = 16
KV_HEADS = 8
HEAD_DIM = 64
TOP = 8
CAP = 24


norm_eps = 1e-05


def slots_of(expert_block, live_rows, experts):
    row_count = expert_block.shape[0]
    chosen = jnp.sum(
        (expert_block[:, :, None] == jnp.arange(experts)[None, None, :]).astype(jnp.float32), axis=1
    )
    member = chosen * live_rows[:, None]
    lower = (jnp.arange(row_count)[None, :] < jnp.arange(row_count)[:, None]).astype(jnp.bfloat16)
    rank = jnp.dot(lower, member.astype(jnp.bfloat16), preferred_element_type=jnp.float32)
    kept = member * (rank < CAP).astype(jnp.float32)
    slot_match = (rank.T[:, None, :] == jnp.arange(CAP, dtype=jnp.float32)[None, :, None]).astype(
        jnp.float32
    )
    dispatch = kept.T[:, None, :] * slot_match
    return (dispatch, kept, chosen, rank)


def axis_bits(size):
    return size.bit_length() - 1


def span(bits):
    masks = [0]
    for bit in bits:
        masks = masks + [mask | (1 << bit) for mask in masks]
    return masks


def dimension_bits(sizes):
    dp_bits, fsdp_bits = (axis_bits(sizes[0]), axis_bits(sizes[1]))
    x_bits = list(range(fsdp_bits))
    high = [fsdp_bits + bit for bit in range(dp_bits - 1, 0, -1)]
    return {"x": x_bits, "z": high[:-1], "y": high[-1:], "c": [fsdp_bits] if dp_bits else []}


def bit_order(sizes, letters):
    bits = dimension_bits(sizes)
    return [bit for letter in letters for bit in bits[letter]]


class Cube:
    def __init__(self, sizes):
        self.sizes = sizes
        self.dp = lax.axis_index("dp")
        self.fsdp = lax.axis_index("fsdp")
        self.me = self.dp * sizes[1] + self.fsdp
        self.fsdp_bits = axis_bits(sizes[1])
        self.bits = axis_bits(sizes[0]) + self.fsdp_bits
        self.flips = [
            (1 - 2 * ((self.me // (1 << bit)) % 2)) * (1 << bit) for bit in range(self.bits)
        ]

    def block(self, mask):
        index = self.me
        for bit, flip in enumerate(self.flips):
            if mask >> bit & 1:
                index = index + flip
        return index

    def device(self, mask):
        other = self.block(mask)
        return {"dp": other // self.sizes[1], "fsdp": other % self.sizes[1]}

    def dp_masks(self):
        masks = [part << self.fsdp_bits for part in range(1, self.sizes[0])]
        return sorted(masks, reverse=True)

    def fsdp_masks(self):
        return list(range(1, self.sizes[1]))

    def greet(self, masks):
        barrier = pltpu.get_barrier_semaphore()
        for mask in masks:
            pl.semaphore_signal(
                barrier, inc=1, device_id=self.device(mask), device_id_type=pl.DeviceIdType.MESH
            )
        pl.semaphore_wait(barrier, len(masks))

    def send(self, source, target, send_sem, recv_sem, mask):
        copy = pltpu.make_async_remote_copy(
            src_ref=source,
            dst_ref=target,
            send_sem=send_sem,
            recv_sem=recv_sem,
            device_id=self.device(mask),
            device_id_type=pl.DeviceIdType.MESH,
        )
        copy.start()
        return copy


def link_of(sizes, bit):
    for letter, bits in dimension_bits(sizes).items():
        if bit in bits:
            return letter
    return "c"


def hop_time(sizes, bit, volume):
    bits = dimension_bits(sizes)
    if bit in bits["c"]:
        return volume / 6.0
    return volume * (1.5 if bit in bits["z"][:-1] else 1.0)


def gather_plan(sizes, orders, volumes, fills, lag, lead):
    free = {}
    known = [{0: 0.0} for _ in orders]
    waiting = []
    for which, order in enumerate(orders):
        for stage, bit in enumerate(order):
            for mask in span(order[:stage]):
                waiting.append((which, mask, bit, len(order) - stage))
    queues = {}
    for at, (link, volume) in enumerate(fills):
        queues.setdefault(link, []).append((at, volume))
    plan = []
    while waiting or any(queues.values()):
        best = None
        for item in waiting:
            which, mask, bit, left = item
            if mask in known[which]:
                begin = max(known[which][mask], free.get(link_of(sizes, bit), 0.0))
                rank = (begin, 0, -left, which, mask)
                if best is None or rank < best[0]:
                    best = (rank, item)
        for link, queue in queues.items():
            if queue:
                rank = (max(free.get(link, 0.0), 1e-6), 1, 0, 0, 0)
                if best is None or rank < best[0]:
                    best = (rank, (None, link))
        rank, item = best
        if item[0] is None:
            at, volume = queues[item[1]].pop(0)
            free[item[1]] = rank[0] + volume
            plan.append((rank[0] - lead, len(plan), (None, at, None)))
            continue
        which, mask, bit, _ = item
        end = rank[0] + hop_time(sizes, bit, volumes[which])
        free[link_of(sizes, bit)] = end
        known[which][mask | (1 << bit)] = end + lag
        plan.append((rank[0], len(plan), (which, mask, bit)))
        waiting.remove(item)
    return [step for _, _, step in sorted(plan)]


def scatter_plan(sizes, orders, volumes, lag):
    free = {}
    known = [{} for _ in orders]
    waiting = []
    for which, order in enumerate(orders):
        for stage, bit in enumerate(order):
            for rest in span(order[stage + 1 :]):
                waiting.append((which, stage, rest | (1 << bit)))
    plan = []
    while waiting:
        best = None
        for item in waiting:
            which, stage, mask = item
            needs = [mask | (1 << earlier) for earlier in orders[which][:stage]]
            if any(need not in known[which] for need in needs):
                continue
            bit = orders[which][stage]
            ready = max([known[which][need] for need in needs], default=0.0)
            begin = max(ready, free.get(link_of(sizes, bit), 0.0))
            after = [at for at, later in enumerate(orders[which]) if mask >> later & 1 and at > stage]
            rank = (begin, after[0] if after else len(orders[which]), which, mask)
            if best is None or rank < best[0]:
                best = (rank, item)
        rank, item = best
        which, stage, mask = item
        bit = orders[which][stage]
        end = rank[0] + hop_time(sizes, bit, volumes[which])
        free[link_of(sizes, bit)] = end
        known[which][mask] = end + lag
        plan.append(item)
        waiting.remove(item)
    return plan


def volume_of(shape):
    total = 1
    for size in shape:
        total = total * size
    return total


EXPERT_PIECES = 4
GATHER_LAG = 5.0
GATHER_LEAD = 1.0
GATHER_ORDERS = ("xzyc", "xzyc", "xzyc", "zxyc", "xzyc")
SCATTER_LAG = 1.5
SCATTER_ORDERS = ("zyxc", "xyzc", "zyxc", "zxyc", "zxyc")


def front_kernel(sizes, count, *refs):
    shards, experts, rows = (refs[:count], refs[count : count + 3], refs[count + 3])
    outs = refs[count + 4 :]
    full, wide, rows_out = (outs[:count], outs[count : count + 3], outs[count + 3])
    local_sems, send_sems, recv_sems, wide_send, wide_recv, row_send, row_recv = outs[count + 4 :]
    cube = Cube(sizes)
    singles = [1 << bit for bit in range(cube.bits)]
    cube.greet(sorted(set(singles + cube.dp_masks() + cube.fsdp_masks())))
    own = []
    for which, (source, target) in enumerate(zip(shards, full)):
        own.append((source, target.at[cube.me]))
    for which, (source, target) in enumerate(zip(experts, wide)):
        own.append((source, target.at[cube.fsdp]))
    own.append((rows.at[cube.dp], rows_out.at[cube.dp]))
    pending = []
    fills = []
    letters = dimension_bits(sizes)
    for piece in range(EXPERT_PIECES):
        for which, source in enumerate(experts):
            for mask in cube.fsdp_masks():
                volume = volume_of(source.shape) / EXPERT_PIECES
                fills.append(("x", volume, ("expert", which, mask, piece)))
    for peer in cube.dp_masks():
        link = [letter for letter in "zyc" if any(peer >> bit & 1 for bit in letters[letter])][0]
        fills.append((link, volume_of(rows.shape[1:]), ("row", peer)))

    def fill(kind, *rest):
        if kind == "expert":
            which, mask, piece = rest
            share = experts[which].shape[0] // EXPERT_PIECES
            place = pl.ds(piece * share, share)
            at = mask * EXPERT_PIECES + piece
            return cube.send(
                experts[which].at[place],
                wide[which].at[cube.fsdp, place],
                wide_send.at[which, at],
                wide_recv.at[which, at],
                mask,
            )
        peer = rest[0]
        part = peer >> cube.fsdp_bits
        return cube.send(
            rows.at[cube.block(peer) // sizes[1]],
            rows_out.at[cube.dp],
            row_send.at[part],
            row_recv.at[part],
            peer,
        )

    orders = [bit_order(sizes, letters) for letters in GATHER_ORDERS]
    unit = 46e3 / 2
    plan = gather_plan(
        sizes,
        orders,
        [volume_of(ref.shape) / unit for ref in shards],
        [(link, volume / unit) for link, volume, _ in fills],
        GATHER_LAG,
        GATHER_LEAD,
    )
    copies = [{} for _ in shards]
    arrived = [{0} for _ in shards]
    started = False
    for which, mask, bit in plan:
        if which is None:
            pending.append(fill(*fills[mask][2]))
            continue
        if mask and not started:
            started = True
            for at, (source, target) in enumerate(own):
                own[at] = pltpu.make_async_copy(source, target, local_sems.at[at])
                own[at].start()
        if mask not in arrived[which]:
            copies[which][mask].wait_recv()
            arrived[which].add(mask)
        label = mask | (1 << bit)
        target = full[which]
        copies[which][label] = cube.send(
            target.at[cube.block(mask)] if mask else shards[which],
            target.at[cube.block(mask)],
            send_sems.at[which, label],
            recv_sems.at[which, label],
            1 << bit,
        )
    for which, made in enumerate(copies):
        for label, copy in made.items():
            if label not in arrived[which]:
                copy.wait_recv()
    for copy in pending:
        copy.wait_recv()
    for copy in own:
        copy.wait()
    for made in copies:
        for copy in made.values():
            copy.wait_send()
    for copy in pending:
        copy.wait_send()


def front_gather(sizes, shards, experts, rows):
    blocks = sizes[0] * sizes[1]
    count = len(shards)
    out_shape = [jax.ShapeDtypeStruct((blocks,) + part.shape, part.dtype) for part in shards]
    out_shape += [jax.ShapeDtypeStruct((sizes[1],) + part.shape, part.dtype) for part in experts]
    out_shape += [jax.ShapeDtypeStruct(rows.shape, rows.dtype)]
    dma = pltpu.SemaphoreType.DMA
    return pl.pallas_call(
        lambda *refs: front_kernel(sizes, count, *refs),
        out_shape=tuple(out_shape),
        in_specs=[pl.BlockSpec(memory_space=pltpu.VMEM)] * (count + 4),
        out_specs=(pl.BlockSpec(memory_space=pl.ANY),) * (count + 4),
        scratch_shapes=[
            dma((count + 4,)),
            dma((count, blocks)),
            dma((count, blocks)),
            dma((3, sizes[1] * EXPERT_PIECES)),
            dma((3, sizes[1] * EXPERT_PIECES)),
            dma((sizes[0],)),
            dma((sizes[0],)),
        ],
        compiler_params=pltpu.CompilerParams(
            collective_id=0, has_side_effects=True, vmem_limit_bytes=24 * 1024 * 1024
        ),
        name="front_gather",
    )(*shards, *experts, rows)


def swap_kernel(sizes, count, parts, *refs):
    rows, grads = (refs[:count], refs[count : count + parts])
    outs = refs[count + parts :]
    rows_out, grads_out = (outs[:count], outs[count : count + parts])
    local_sems, row_send, row_recv, part_send, part_recv = outs[count + parts :]
    cube = Cube(sizes)
    cube.greet(cube.dp_masks() + (cube.fsdp_masks() if parts else []))
    pending = []
    for peer in cube.dp_masks():
        part = peer >> cube.fsdp_bits
        for which in range(count):
            pending.append(
                cube.send(
                    rows[which].at[cube.block(peer) // sizes[1]],
                    rows_out[which].at[cube.dp],
                    row_send.at[which, part],
                    row_recv.at[which, part],
                    peer,
                )
            )
    for mask in cube.fsdp_masks() if parts else []:
        for which in range(parts):
            pending.append(
                cube.send(
                    grads[which].at[cube.block(mask) % sizes[1]],
                    grads_out[which].at[mask - 1],
                    part_send.at[which, mask],
                    part_recv.at[which, mask],
                    mask,
                )
            )
    own = []
    for which in range(count):
        own.append(
            pltpu.make_async_copy(
                rows[which].at[cube.dp], rows_out[which].at[cube.dp], local_sems.at[which]
            )
        )
        own[-1].start()
    for copy in pending:
        copy.wait_recv()
    for copy in own:
        copy.wait()
    for copy in pending:
        copy.wait_send()


def swap_rows(sizes, rows, grads, collective_id, name):
    count, parts = (len(rows), len(grads))
    peers = max(sizes[1] - 1, 1)
    out_shape = [jax.ShapeDtypeStruct(part.shape, part.dtype) for part in rows]
    out_shape += [
        jax.ShapeDtypeStruct((peers,) + part.shape[1:], part.dtype) for part in grads
    ]
    dma = pltpu.SemaphoreType.DMA
    return pl.pallas_call(
        lambda *refs: swap_kernel(sizes, count, parts, *refs),
        out_shape=tuple(out_shape),
        in_specs=[pl.BlockSpec(memory_space=pltpu.VMEM)] * (count + parts),
        out_specs=(pl.BlockSpec(memory_space=pl.ANY),) * (count + parts),
        scratch_shapes=[
            dma((count,)),
            dma((count, sizes[0])),
            dma((count, sizes[0])),
            dma((max(parts, 1), sizes[1])),
            dma((max(parts, 1), sizes[1])),
        ],
        compiler_params=pltpu.CompilerParams(
            collective_id=collective_id,
            has_side_effects=True,
            vmem_limit_bytes=24 * 1024 * 1024,
        ),
        name=name,
    )(*rows, *grads)


def scatter_kernel(sizes, count, *refs):
    sources, outs = (refs[:count], refs[count : 2 * count])
    slots, held = (refs[2 * count : 3 * count], refs[3 * count : 4 * count])
    send_sems, recv_sems = refs[4 * count :]
    cube = Cube(sizes)
    cube.greet([1 << bit for bit in range(cube.bits)])
    orders = [bit_order(sizes, letters)[::-1] for letters in SCATTER_ORDERS]
    copies = [{} for _ in sources]
    arrived = [set() for _ in sources]
    places = [{} for _ in sources]

    def total(which, mask, stage):
        value = sources[which][cube.block(mask)].astype(jnp.float32)
        for earlier in orders[which][:stage]:
            label = mask | (1 << earlier)
            copies[which][label].wait_recv()
            value = value + slots[which][label].astype(jnp.float32)
        return value

    for which, stage, mask in scatter_plan(
        sizes, orders, [volume_of(ref.shape) / 23e3 for ref in outs], SCATTER_LAG
    ):
        if stage == 0:
            leaving = sources[which].at[cube.block(mask)]
        else:
            slot = places[which].setdefault(mask, len(places[which]))
            held[which][slot] = total(which, mask, stage).astype(jnp.bfloat16)
            leaving = held[which].at[slot]
        copies[which][mask] = cube.send(
            leaving,
            slots[which].at[mask],
            send_sems.at[which, mask],
            recv_sems.at[which, mask],
            1 << orders[which][stage],
        )
    for which in range(count):
        outs[which][...] = total(which, 0, len(orders[which]))
    for made in copies:
        for copy in made.values():
            copy.wait_send()


def scatter_rows(sizes, packed):
    blocks = sizes[0] * sizes[1]
    count = len(packed)
    shapes = [part.shape[1:] for part in packed]
    dma = pltpu.SemaphoreType.DMA
    return pl.pallas_call(
        lambda *refs: scatter_kernel(sizes, count, *refs),
        out_shape=tuple(jax.ShapeDtypeStruct(shape, jnp.float32) for shape in shapes),
        in_specs=[pl.BlockSpec(memory_space=pltpu.VMEM)] * count,
        out_specs=(pl.BlockSpec(memory_space=pltpu.VMEM),) * count,
        scratch_shapes=[pltpu.VMEM((blocks,) + shape, jnp.bfloat16) for shape in shapes]
        + [pltpu.VMEM((blocks // 2,) + shape, jnp.bfloat16) for shape in shapes]
        + [dma((count, blocks)), dma((count, blocks))],
        compiler_params=pltpu.CompilerParams(
            collective_id=3, has_side_effects=True, vmem_limit_bytes=48 * 1024 * 1024
        ),
        name="scatter_rows",
    )(*packed)


def lanes_of(shape):
    return lax.broadcasted_iota(jnp.int32, shape, 1)


def rows_of(shape):
    return lax.broadcasted_iota(jnp.int32, shape, 0)


def dot(left, right):
    return jnp.dot(left, right, preferred_element_type=jnp.float32)


def dot_nt(left, right):
    return lax.dot_general(
        left, right, (((1,), (1,)), ((), ())), preferred_element_type=jnp.float32
    )


def dot_tn(left, right):
    return lax.dot_general(
        left, right, (((0,), (0,)), ((), ())), preferred_element_type=jnp.float32
    )


def half(values):
    return values.astype(jnp.bfloat16)


def wide(values):
    return values.astype(jnp.float32)


def masks_of(doc_ref):
    count = doc_ref.shape[1]
    doc_row = jnp.broadcast_to(doc_ref[...].astype(jnp.float32), (count, count))
    doc_col = doc_row.T
    same = doc_row == doc_col
    row, lane = (rows_of((count, count)), lanes_of((count, count)))
    position = jnp.sum(jnp.where(same & (lane < row), 1.0, 0.0), axis=1, keepdims=True)
    allowed = same & (lane <= row)
    live = jnp.where(doc_col[:, :1] < count, 1.0, 0.0)
    return (position, allowed, live)


def slots_in_kernel(ids_ref, live, experts):
    count = ids_ref.shape[0]
    lane = lanes_of((count, 128))
    ids = ids_ref[...]
    chosen = jnp.zeros((count, 128), jnp.float32)
    for top in range(ids.shape[1]):
        chosen = chosen + jnp.where(ids[:, top : top + 1] == lane, 1.0, 0.0)
    member = chosen * live
    lower = jnp.where(lanes_of((count, count)) < rows_of((count, count)), 1.0, 0.0)
    rank = dot(half(lower), half(member))
    kept = jnp.where(rank < CAP, member, 0.0)
    place = jnp.where(kept > 0.0, rank, -1.0).T[:experts]
    slot = lax.broadcasted_iota(jnp.int32, (experts, CAP, count), 1).astype(jnp.float32)
    dispatch = jnp.where(place[:, None, :] == slot, 1.0, 0.0)
    return (chosen, dispatch)


def rope_in_kernel(position):
    lane = lanes_of((position.shape[0], 128))
    half_dim = HEAD_DIM // 2
    step = (lane % half_dim).astype(jnp.float32)
    freqs = jnp.exp(-jnp.log(10000.0) * (2.0 * step / HEAD_DIM))
    angle = position * freqs
    first = lane % HEAD_DIM < half_dim
    sinusoid = jnp.sin(angle)
    return (jnp.cos(angle), jnp.where(first, -sinusoid, sinusoid), first)


def swap_halves(values, first):
    width = values.shape[1]
    half_dim = HEAD_DIM // 2
    return jnp.where(
        first, pltpu.roll(values, width - half_dim, 1), pltpu.roll(values, half_dim, 1)
    )


def doubled(tile, odd):
    front = lanes_of(tile.shape) < HEAD_DIM
    rolled = pltpu.roll(tile, HEAD_DIM, 1)
    return half(jnp.where(front, rolled, tile) if odd else jnp.where(front, tile, rolled))


def stacked(tile):
    front = lanes_of(tile.shape) < HEAD_DIM
    return half(
        jnp.concatenate([jnp.where(front, tile, 0.0), jnp.where(front, 0.0, tile)], axis=0)
    )


def unstacked(pair):
    count = pair.shape[0] // 2
    front = lanes_of((count, pair.shape[1])) < HEAD_DIM
    return jnp.where(front, pair[:count], pair[count:])


def tile_of(at):
    return slice(128 * at, 128 * at + 128)


def small_rows(small_ref, experts):
    pick = jnp.where(lanes_of((8, 128)) == rows_of((8, 128)) + experts, 1.0, 0.0)
    picked = dot_nt(half(pick), small_ref[...])
    return (picked[0:1], picked[1:2])


def norm_in_kernel(values):
    scale_row = lax.rsqrt(jnp.mean(values * values, axis=1, keepdims=True) + norm_eps)
    return (values * scale_row, scale_row)


def forward_kernel(
    experts,
    hidden_ref,
    doc_ref,
    ids_ref,
    query_ref,
    key_ref,
    value_ref,
    output_ref,
    small_ref,
    rows_out,
    mid_out,
    q_out,
    k_out,
    v_out,
    p_out,
    o_out,
    routed_out,
    gates_out,
):
    scale = HEAD_DIM ** (-0.5)
    position, allowed, live = masks_of(doc_ref)
    chosen, dispatch = slots_in_kernel(ids_ref, live, experts)
    cosine, sinusoid, first = rope_in_kernel(position)
    gain_one, gain_two = small_rows(small_ref, experts)
    resid = wide(hidden_ref[...])
    normed, _ = norm_in_kernel(resid)
    h1 = half(normed * gain_one)
    key_raw = dot(h1, key_ref[...])
    for at in range(key_raw.shape[1] // 128):
        part = key_raw[:, tile_of(at)]
        k_out[:, tile_of(at)] = half(part * cosine + swap_halves(part, first) * sinusoid)
    v_out[...] = half(dot(h1, value_ref[...]))
    query_raw = dot(h1, query_ref[...])
    both = jnp.concatenate([allowed, allowed], axis=0)
    for head in range(KV_HEADS):
        part = query_raw[:, tile_of(head)]
        turned = half(part * cosine + swap_halves(part, first) * sinusoid)
        q_out[:, tile_of(head)] = turned
        keys = doubled(wide(k_out[:, tile_of(head // 2)]), head % 2)
        values = doubled(wide(v_out[:, tile_of(head // 2)]), head % 2)
        scores = dot_nt(stacked(wide(turned)), keys) * scale
        raised = jnp.where(both, jnp.exp(scores), 0.0)
        total = jnp.log(jnp.sum(raised, axis=1, keepdims=True))
        probs = jnp.where(both, jnp.exp(scores - total), 0.0)
        p_out[head] = probs
        o_out[:, tile_of(head)] = half(unstacked(dot(half(probs), values)) * live)
    mid = resid + dot(o_out[...], output_ref[...])
    mid_out[...] = mid
    normed_two, _ = norm_in_kernel(mid)
    h2 = half(normed_two * gain_two)
    routed_out[...] = h2
    logits = dot(h2, small_ref[...])
    raised = jnp.where(chosen > 0.0, jnp.exp(logits), 0.0)
    gates = raised / jnp.sum(raised, axis=1, keepdims=True)
    gates_t = gates.T[:experts]
    gates_out[...] = gates_t
    slots = experts * CAP
    one_hot = half(dispatch.reshape(slots, -1))
    slot_gate = jnp.sum(
        (dispatch * gates_t[:, None, :]).reshape(slots, -1), axis=1, keepdims=True
    )
    high = wide(half(slot_gate))
    middle = wide(half(slot_gate - high))
    low = slot_gate - high - middle
    lane = lanes_of((slots, 128))
    packed = jnp.where(
        lane == 0, high, jnp.where(lane == 1, middle, jnp.where(lane == 2, low, 0.0))
    )
    width = h2.shape[1]
    sent = dot(one_hot, h2)
    for e in range(experts):
        rows_out[e, :, :width] = half(sent[e * CAP : (e + 1) * CAP])
        rows_out[e, :, width:] = half(packed[e * CAP : (e + 1) * CAP])


def expert_kernel(rows_ref, grads_ref, gate_ref, up_ref, down_ref, out_ref, back_ref, *grads_out):
    width = grads_ref.shape[1]
    rows = rows_ref[:, :width]
    slot_gate = jnp.sum(wide(rows_ref[:, width:]), axis=1, keepdims=True)
    grad_rows = half(slot_gate * wide(grads_ref[...]))
    gate_pre = dot(rows, gate_ref[...])
    up_pre = dot(rows, up_ref[...])
    sigmoid_gate = 1.0 / (1.0 + jnp.exp(-gate_pre))
    act = half(gate_pre * sigmoid_gate * up_pre)
    out_ref[...] = half(dot(act, down_ref[...]))
    grad_act = dot_nt(grad_rows, down_ref[...])
    grad_up = half(grad_act * gate_pre * sigmoid_gate)
    grad_gate = half(grad_act * up_pre * sigmoid_gate * (1.0 + gate_pre * (1.0 - sigmoid_gate)))
    back_ref[...] = half(dot_nt(grad_gate, gate_ref[...]) + dot_nt(grad_up, up_ref[...]))
    made = (dot_tn(rows, grad_gate), dot_tn(rows, grad_up), dot_tn(act, grad_rows))
    for which, value in enumerate(made):
        grads_out[which][...] = value
        grads_out[which + 3][...] = half(value)


def backward_kernel(
    experts,
    hidden_ref,
    doc_ref,
    ids_ref,
    grad_ref,
    query_ref,
    key_ref,
    value_ref,
    output_ref,
    small_ref,
    mid_ref,
    q_ref,
    k_ref,
    v_ref,
    p_ref,
    o_ref,
    routed_ref,
    gates_ref,
    back_ref,
    slots_ref,
    layer_out,
    input_out,
    query_out,
    key_out,
    value_out,
    output_out,
    small_out,
    dq_ref,
    dk_ref,
    dv_ref,
):
    scale = HEAD_DIM ** (-0.5)
    position, _, live = masks_of(doc_ref)
    _, dispatch = slots_in_kernel(ids_ref, live, experts)
    cosine, sinusoid, first = rope_in_kernel(position)
    gain_one, gain_two = small_rows(small_ref, experts)
    slots = experts * CAP
    count = doc_ref.shape[1]
    gates = gates_ref[...]
    combine = (dispatch * gates[:, None, :]).reshape(slots, count).T
    combine_high = half(combine)
    combine_low = half(combine - wide(combine_high))
    flat = dispatch.reshape(slots, count)
    flat_t = half(flat.T)
    mid = mid_ref[...]
    out_rows = back_ref[...]
    layer_out[...] = half(mid + (dot(combine_high, out_rows) + dot(combine_low, out_rows)))
    row_dots = dot_nt(out_rows, grad_ref[...])
    grad_gates = jnp.sum((flat * row_dots).reshape(experts, CAP, count), axis=1)
    grad_logits = gates * (grad_gates - jnp.sum(gates * grad_gates, axis=0, keepdims=True))
    logit_rows = jnp.concatenate(
        [grad_logits, jnp.zeros((128 - experts, count), jnp.float32)], axis=0
    )
    logits_t = half(logit_rows.T)
    grad_router = dot(half(logit_rows), routed_ref[...])
    grad_routed = dot(flat_t, slots_ref[...]) + dot_nt(logits_t, small_ref[...])
    normed_two, scale_two = norm_in_kernel(mid)
    scaled = grad_routed * gain_two
    inner = jnp.mean(scaled * normed_two, axis=1, keepdims=True)
    grad_gain_two = jnp.sum(grad_routed * normed_two, axis=0, keepdims=True)
    grad_mid = wide(grad_ref[...]) + scale_two * (scaled - normed_two * inner)
    grad_mid_b = half(grad_mid)
    output_out[...] = half(dot_tn(o_ref[...], grad_mid_b))
    grad_mixed = half(dot_nt(grad_mid_b, output_ref[...]) * live)
    front = lanes_of((count, 128)) < HEAD_DIM
    pair = {}
    for head in range(KV_HEADS):
        keys = doubled(wide(k_ref[:, tile_of(head // 2)]), head % 2)
        values = doubled(wide(v_ref[:, tile_of(head // 2)]), head % 2)
        queries = stacked(wide(q_ref[:, tile_of(head)]))
        mixed = stacked(wide(grad_mixed[:, tile_of(head)]))
        probs = p_ref[head]
        grad_probs = dot_nt(mixed, values)
        delta = jnp.sum(probs * grad_probs, axis=1, keepdims=True)
        grad_scores = half(probs * (grad_probs - delta) * scale)
        part = unstacked(dot(grad_scores, keys))
        dq_ref[:, tile_of(head)] = half(part * cosine - swap_halves(part, first) * sinusoid)
        grad_key = dot_tn(grad_scores, queries)
        grad_value = dot_tn(half(probs), mixed)
        pair[head % 2] = (
            grad_key + pltpu.roll(grad_key, HEAD_DIM, 1),
            grad_value + pltpu.roll(grad_value, HEAD_DIM, 1),
        )
        if head % 2:
            part = jnp.where(front, pair[0][0], pair[1][0])
            dk_ref[:, tile_of(head // 2)] = half(
                part * cosine - swap_halves(part, first) * sinusoid
            )
            dv_ref[:, tile_of(head // 2)] = half(jnp.where(front, pair[0][1], pair[1][1]))
    resid = wide(hidden_ref[...])
    normed_one, scale_one = norm_in_kernel(resid)
    h1 = half(normed_one * gain_one)
    query_out[...] = half(dot_tn(h1, dq_ref[...]))
    key_out[...] = half(dot_tn(h1, dk_ref[...]))
    value_out[...] = half(dot_tn(h1, dv_ref[...]))
    grad_normed = dot_nt(dq_ref[...], query_ref[...])
    grad_normed = grad_normed + dot_nt(dk_ref[...], key_ref[...])
    grad_normed = grad_normed + dot_nt(dv_ref[...], value_ref[...])
    scaled = grad_normed * gain_one
    inner = jnp.mean(scaled * normed_one, axis=1, keepdims=True)
    grad_gain_one = jnp.sum(grad_normed * normed_one, axis=0, keepdims=True)
    input_out[...] = half(grad_mid + scale_one * (scaled - normed_one * inner))
    row = rows_of(grad_router.shape)
    small = jnp.where(
        row < experts,
        grad_router,
        jnp.where(row == experts, grad_gain_one, jnp.where(row == experts + 1, grad_gain_two, 0.0)),
    )
    small_out[...] = half(small.T)


def plain_call(kernel, name, outs, scratch, *args):
    return pl.pallas_call(
        kernel,
        out_shape=tuple(jax.ShapeDtypeStruct(shape, dtype) for shape, dtype in outs),
        in_specs=[pl.BlockSpec(memory_space=pltpu.VMEM)] * len(args),
        out_specs=(pl.BlockSpec(memory_space=pltpu.VMEM),) * len(outs),
        scratch_shapes=[pltpu.VMEM(shape, dtype) for shape, dtype in scratch],
        compiler_params=pltpu.CompilerParams(vmem_limit_bytes=60 * 1024 * 1024),
        name=name,
    )(*args)


def shards(
    sizes,
    hidden_in,
    doc_id,
    expert_ids,
    out_grad,
    attn_gain,
    query_weight,
    key_weight,
    value_weight,
    output_weight,
    ffn_gain,
    router_weight,
    expert_gate,
    expert_up,
    expert_down,
):
    rows, width = hidden_in.shape
    experts = router_weight.shape[1]
    blocks = sizes[0] * sizes[1]
    query_width, key_width = (query_weight.shape[1], key_weight.shape[1])
    hidden_units = expert_gate.shape[2]
    small = jnp.concatenate([router_weight, attn_gain[:, None], ffn_gain[:, None]], axis=1)
    small = jnp.pad(small, ((0, 0), (0, 128 - small.shape[1])))
    doc_row = doc_id.reshape(1, rows)
    slots = experts * CAP
    bf16, f32 = (jnp.bfloat16, jnp.float32)
    live_rows = (doc_id < rows).astype(f32)
    dispatch, _, _, _ = slots_of(expert_ids, live_rows, experts)
    pulled_b = jnp.einsum(
        "ecr,rd->ecd", dispatch.astype(bf16), out_grad, preferred_element_type=f32
    ).astype(bf16)
    gathered = front_gather(
        sizes,
        (query_weight, key_weight, value_weight, output_weight, small),
        (expert_gate[0], expert_up[0], expert_down[0]),
        pulled_b,
    )
    dense = [part.reshape(-1, part.shape[2]) for part in gathered[:5]]
    wide_experts = [part.reshape(-1, part.shape[2]) for part in gathered[5:8]]
    saved = plain_call(
        functools.partial(forward_kernel, experts),
        "forward",
        [
            ((experts, CAP, width + 128), bf16),
            ((rows, width), f32),
            ((rows, query_width), bf16),
            ((rows, key_width), bf16),
            ((rows, key_width), bf16),
            ((KV_HEADS, 2 * rows, rows), f32),
            ((rows, query_width), bf16),
            ((rows, width), bf16),
            ((experts, rows), f32),
        ],
        [],
        hidden_in,
        doc_row,
        expert_ids,
        *dense,
    )
    (recv,) = swap_rows(sizes, (saved[0],), (), 1, "swap_out")
    made = plain_call(
        expert_kernel,
        "experts",
        [((slots, width), bf16)] * 2
        + [((width, hidden_units), f32)] * 2
        + [((hidden_units, width), f32)]
        + [((width, hidden_units), bf16)] * 2
        + [((hidden_units, width), bf16)],
        [],
        recv.reshape(slots, -1),
        gathered[8].reshape(slots, width),
        *wide_experts,
    )
    swapped = swap_rows(
        sizes,
        [part.reshape(experts, CAP, width) for part in made[:2]],
        [part.reshape((sizes[1], -1) + part.shape[1:]) for part in made[5:]],
        2,
        "swap_back",
    )
    own = lax.axis_index("fsdp")
    expert_grads = [
        lax.dynamic_index_in_dim(
            mine.reshape((sizes[1], -1) + mine.shape[1:]), own, axis=0, keepdims=True
        )
        + jnp.sum(other.astype(f32), axis=0, keepdims=True)
        for mine, other in zip(made[2:5], swapped[2:])
    ]
    results = plain_call(
        functools.partial(backward_kernel, experts),
        "backward",
        [
            ((rows, width), bf16),
            ((rows, width), bf16),
            ((width, query_width), bf16),
            ((width, key_width), bf16),
            ((width, key_width), bf16),
            ((query_width, width), bf16),
            ((width, 128), bf16),
        ],
        [((rows, query_width), bf16), ((rows, key_width), bf16), ((rows, key_width), bf16)],
        hidden_in,
        doc_row,
        expert_ids,
        out_grad,
        *dense,
        *saved[1:],
        swapped[0].reshape(slots, width),
        swapped[1].reshape(slots, width),
    )
    own_query, own_key, own_value, own_output, own_small = scatter_rows(
        sizes, [part.reshape(blocks, -1, part.shape[1]) for part in results[2:]]
    )
    return (
        results[0],
        results[1],
        own_small[:, experts],
        own_query,
        own_key,
        own_value,
        own_output,
        own_small[:, experts + 1],
        own_small[:, :experts],
        expert_grads[0],
        expert_grads[1],
        expert_grads[2],
    )


def solution(mesh):
    in_specs = (
        P(("dp", "fsdp"), None),
        P(("dp", "fsdp")),
        P(("dp", "fsdp"), None),
        P(("dp", "fsdp"), None),
        P(("dp", "fsdp")),
        P(("dp", "fsdp"), None),
        P(("dp", "fsdp"), None),
        P(("dp", "fsdp"), None),
        P(("dp", "fsdp"), None),
        P(("dp", "fsdp")),
        P(("dp", "fsdp"), None),
        P("dp", "fsdp", None),
        P("dp", "fsdp", None),
        P("dp", "fsdp", None),
    )
    out_specs = (
        P(("dp", "fsdp"), None),
        P(("dp", "fsdp"), None),
        P(("dp", "fsdp")),
        P(("dp", "fsdp"), None),
        P(("dp", "fsdp"), None),
        P(("dp", "fsdp"), None),
        P(("dp", "fsdp"), None),
        P(("dp", "fsdp")),
        P(("dp", "fsdp"), None),
        P("dp", "fsdp", None),
        P("dp", "fsdp", None),
        P("dp", "fsdp", None),
    )
    sizes = (mesh.shape["dp"], mesh.shape["fsdp"])
    body = functools.partial(shards, sizes)
    return jax.shard_map(body, mesh=mesh, in_specs=in_specs, out_specs=out_specs, check_vma=False)
```

```python
import functools

import jax
import jax.numpy as jnp
from jax import lax
from jax.experimental import pallas as pl
from jax.experimental.pallas import tpu as pltpu
from jax.sharding import PartitionSpec as P

HEADS = 16
KV_HEADS = 8
HEAD_DIM = 64
TOP = 8
CAP = 24


norm_eps = 1e-05


def slots_of(expert_block, live_rows, experts):
    row_count = expert_block.shape[0]
    chosen = jnp.sum(
        (expert_block[:, :, None] == jnp.arange(experts)[None, None, :]).astype(jnp.float32), axis=1
    )
    member = chosen * live_rows[:, None]
    lower = (jnp.arange(row_count)[None, :] < jnp.arange(row_count)[:, None]).astype(jnp.bfloat16)
    rank = jnp.dot(lower, member.astype(jnp.bfloat16), preferred_element_type=jnp.float32)
    kept = member * (rank < CAP).astype(jnp.float32)
    slot_match = (rank.T[:, None, :] == jnp.arange(CAP, dtype=jnp.float32)[None, :, None]).astype(
        jnp.float32
    )
    dispatch = kept.T[:, None, :] * slot_match
    return (dispatch, kept, chosen, rank)


def axis_bits(size):
    return size.bit_length() - 1


def span(bits):
    masks = [0]
    for bit in bits:
        masks = masks + [mask | (1 << bit) for mask in masks]
    return masks


def dimension_bits(sizes):
    dp_bits, fsdp_bits = (axis_bits(sizes[0]), axis_bits(sizes[1]))
    x_bits = list(range(fsdp_bits))
    high = [fsdp_bits + bit for bit in range(dp_bits - 1, 0, -1)]
    return {"x": x_bits, "z": high[:-1], "y": high[-1:], "c": [fsdp_bits] if dp_bits else []}


def bit_order(sizes, letters):
    bits = dimension_bits(sizes)
    return [bit for letter in letters for bit in bits[letter]]


class Cube:
    def __init__(self, sizes):
        self.sizes = sizes
        self.dp = lax.axis_index("dp")
        self.fsdp = lax.axis_index("fsdp")
        self.me = self.dp * sizes[1] + self.fsdp
        self.fsdp_bits = axis_bits(sizes[1])
        self.bits = axis_bits(sizes[0]) + self.fsdp_bits
        self.flips = [
            (1 - 2 * ((self.me // (1 << bit)) % 2)) * (1 << bit) for bit in range(self.bits)
        ]

    def block(self, mask):
        index = self.me
        for bit, flip in enumerate(self.flips):
            if mask >> bit & 1:
                index = index + flip
        return index

    def device(self, mask):
        other = self.block(mask)
        return {"dp": other // self.sizes[1], "fsdp": other % self.sizes[1]}

    def dp_masks(self):
        masks = [part << self.fsdp_bits for part in range(1, self.sizes[0])]
        return sorted(masks, reverse=True)

    def fsdp_masks(self):
        return list(range(1, self.sizes[1]))

    def greet(self, masks):
        barrier = pltpu.get_barrier_semaphore()
        for mask in masks:
            pl.semaphore_signal(
                barrier, inc=1, device_id=self.device(mask), device_id_type=pl.DeviceIdType.MESH
            )
        pl.semaphore_wait(barrier, len(masks))

    def send(self, source, target, send_sem, recv_sem, mask):
        copy = pltpu.make_async_remote_copy(
            src_ref=source,
            dst_ref=target,
            send_sem=send_sem,
            recv_sem=recv_sem,
            device_id=self.device(mask),
            device_id_type=pl.DeviceIdType.MESH,
        )
        copy.start()
        return copy


def link_of(sizes, bit):
    for letter, bits in dimension_bits(sizes).items():
        if bit in bits:
            return letter
    return "c"


def hop_time(sizes, bit, volume):
    bits = dimension_bits(sizes)
    if bit in bits["c"]:
        return volume / 6.0
    return volume * (1.5 if bit in bits["z"][:-1] else 1.0)


def gather_plan(sizes, orders, volumes, fills, lag, lead):
    free = {}
    known = [{0: 0.0} for _ in orders]
    waiting = []
    for which, order in enumerate(orders):
        for stage, bit in enumerate(order):
            for mask in span(order[:stage]):
                waiting.append((which, mask, bit, len(order) - stage))
    queues = {}
    for at, (link, volume) in enumerate(fills):
        queues.setdefault(link, []).append((at, volume))
    plan = []
    while waiting or any(queues.values()):
        best = None
        for item in waiting:
            which, mask, bit, left = item
            if mask in known[which]:
                begin = max(known[which][mask], free.get(link_of(sizes, bit), 0.0))
                rank = (begin, 0, -left, which, mask)
                if best is None or rank < best[0]:
                    best = (rank, item)
        for link, queue in queues.items():
            if queue:
                rank = (max(free.get(link, 0.0), 1e-6) + queue[0][1], 1, 0, 0, 0)
                if best is None or rank < best[0]:
                    best = (rank, (None, link))
        rank, item = best
        if item[0] is None:
            at, volume = queues[item[1]].pop(0)
            free[item[1]] = rank[0]
            plan.append((rank[0] - volume - lead, len(plan), (None, at, None)))
            continue
        which, mask, bit, _ = item
        end = rank[0] + hop_time(sizes, bit, volumes[which])
        free[link_of(sizes, bit)] = end
        known[which][mask | (1 << bit)] = end + lag
        plan.append((rank[0], len(plan), (which, mask, bit)))
        waiting.remove(item)
    return [step for _, _, step in sorted(plan)]


def scatter_plan(sizes, orders, volumes, lag):
    free = {}
    known = [{} for _ in orders]
    waiting = []
    for which, order in enumerate(orders):
        for stage, bit in enumerate(order):
            for rest in span(order[stage + 1 :]):
                waiting.append((which, stage, rest | (1 << bit)))
    plan = []
    while waiting:
        best = None
        for item in waiting:
            which, stage, mask = item
            needs = [mask | (1 << earlier) for earlier in orders[which][:stage]]
            if any(need not in known[which] for need in needs):
                continue
            bit = orders[which][stage]
            ready = max([known[which][need] for need in needs], default=0.0)
            begin = max(ready, free.get(link_of(sizes, bit), 0.0))
            after = [at for at, later in enumerate(orders[which]) if mask >> later & 1 and at > stage]
            rank = (begin, after[0] if after else len(orders[which]), which, mask)
            if best is None or rank < best[0]:
                best = (rank, item)
        rank, item = best
        which, stage, mask = item
        bit = orders[which][stage]
        end = rank[0] + hop_time(sizes, bit, volumes[which])
        free[link_of(sizes, bit)] = end
        known[which][mask] = end + lag
        plan.append(item)
        waiting.remove(item)
    return plan


def volume_of(shape):
    total = 1
    for size in shape:
        total = total * size
    return total


EXPERT_PIECES = 4
GATHER_LAG = 5.0
GATHER_LEAD = 1.0
GATHER_ORDERS = ("xzyc", "xzyc", "xzyc", "zxyc", "xzyc")
SCATTER_LAG = 1.5
SCATTER_ORDERS = ("zyxc", "xyzc", "zyxc", "zxyc", "zxyc")


def front_kernel(sizes, count, *refs):
    shards, experts, rows = (refs[:count], refs[count : count + 3], refs[count + 3])
    outs = refs[count + 4 :]
    full, wide, rows_out = (outs[:count], outs[count : count + 3], outs[count + 3])
    local_sems, send_sems, recv_sems, wide_send, wide_recv, row_send, row_recv = outs[count + 4 :]
    cube = Cube(sizes)
    singles = [1 << bit for bit in range(cube.bits)]
    cube.greet(sorted(set(singles + cube.dp_masks() + cube.fsdp_masks())))
    own = []
    for which, (source, target) in enumerate(zip(shards, full)):
        own.append((source, target.at[cube.me]))
    for which, (source, target) in enumerate(zip(experts, wide)):
        own.append((source, target.at[cube.fsdp]))
    own.append((rows.at[cube.dp], rows_out.at[cube.dp]))
    pending = []
    fills = []
    letters = dimension_bits(sizes)
    for piece in range(EXPERT_PIECES):
        for which, source in enumerate(experts):
            for mask in cube.fsdp_masks():
                volume = volume_of(source.shape) / EXPERT_PIECES
                fills.append(("x", volume, ("expert", which, mask, piece)))
    for peer in cube.dp_masks():
        link = [letter for letter in "zyc" if any(peer >> bit & 1 for bit in letters[letter])][0]
        fills.append((link, volume_of(rows.shape[1:]), ("row", peer)))

    def fill(kind, *rest):
        if kind == "expert":
            which, mask, piece = rest
            share = experts[which].shape[0] // EXPERT_PIECES
            place = pl.ds(piece * share, share)
            at = mask * EXPERT_PIECES + piece
            return cube.send(
                experts[which].at[place],
                wide[which].at[cube.fsdp, place],
                wide_send.at[which, at],
                wide_recv.at[which, at],
                mask,
            )
        peer = rest[0]
        part = peer >> cube.fsdp_bits
        return cube.send(
            rows.at[cube.block(peer) // sizes[1]],
            rows_out.at[cube.dp],
            row_send.at[part],
            row_recv.at[part],
            peer,
        )

    orders = [bit_order(sizes, letters) for letters in GATHER_ORDERS]
    unit = 46e3 / 2
    plan = gather_plan(
        sizes,
        orders,
        [volume_of(ref.shape) / unit for ref in shards],
        [(link, volume / unit) for link, volume, _ in fills],
        GATHER_LAG,
        GATHER_LEAD,
    )
    copies = [{} for _ in shards]
    arrived = [{0} for _ in shards]
    started = False
    for which, mask, bit in plan:
        if which is None:
            pending.append(fill(*fills[mask][2]))
            continue
        if mask and not started:
            started = True
            for at, (source, target) in enumerate(own):
                own[at] = pltpu.make_async_copy(source, target, local_sems.at[at])
                own[at].start()
        if mask not in arrived[which]:
            copies[which][mask].wait_recv()
            arrived[which].add(mask)
        label = mask | (1 << bit)
        target = full[which]
        copies[which][label] = cube.send(
            target.at[cube.block(mask)] if mask else shards[which],
            target.at[cube.block(mask)],
            send_sems.at[which, label],
            recv_sems.at[which, label],
            1 << bit,
        )
    for which, made in enumerate(copies):
        for label, copy in made.items():
            if label not in arrived[which]:
                copy.wait_recv()
    for copy in pending:
        copy.wait_recv()
    for copy in own:
        copy.wait()
    for made in copies:
        for copy in made.values():
            copy.wait_send()
    for copy in pending:
        copy.wait_send()


def front_gather(sizes, shards, experts, rows):
    blocks = sizes[0] * sizes[1]
    count = len(shards)
    out_shape = [jax.ShapeDtypeStruct((blocks,) + part.shape, part.dtype) for part in shards]
    out_shape += [jax.ShapeDtypeStruct((sizes[1],) + part.shape, part.dtype) for part in experts]
    out_shape += [jax.ShapeDtypeStruct(rows.shape, rows.dtype)]
    dma = pltpu.SemaphoreType.DMA
    return pl.pallas_call(
        lambda *refs: front_kernel(sizes, count, *refs),
        out_shape=tuple(out_shape),
        in_specs=[pl.BlockSpec(memory_space=pltpu.VMEM)] * (count + 4),
        out_specs=(pl.BlockSpec(memory_space=pl.ANY),) * (count + 4),
        scratch_shapes=[
            dma((count + 4,)),
            dma((count, blocks)),
            dma((count, blocks)),
            dma((3, sizes[1] * EXPERT_PIECES)),
            dma((3, sizes[1] * EXPERT_PIECES)),
            dma((sizes[0],)),
            dma((sizes[0],)),
        ],
        compiler_params=pltpu.CompilerParams(
            collective_id=0, has_side_effects=True, vmem_limit_bytes=24 * 1024 * 1024
        ),
        name="front_gather",
    )(*shards, *experts, rows)


def swap_kernel(sizes, count, parts, *refs):
    rows, grads = (refs[:count], refs[count : count + parts])
    outs = refs[count + parts :]
    rows_out, grads_out = (outs[:count], outs[count : count + parts])
    local_sems, row_send, row_recv, part_send, part_recv = outs[count + parts :]
    cube = Cube(sizes)
    cube.greet(cube.dp_masks() + (cube.fsdp_masks() if parts else []))
    pending = []
    for peer in cube.dp_masks():
        part = peer >> cube.fsdp_bits
        for which in range(count):
            pending.append(
                cube.send(
                    rows[which].at[cube.block(peer) // sizes[1]],
                    rows_out[which].at[cube.dp],
                    row_send.at[which, part],
                    row_recv.at[which, part],
                    peer,
                )
            )
    for mask in cube.fsdp_masks() if parts else []:
        for which in range(parts):
            pending.append(
                cube.send(
                    grads[which].at[cube.block(mask) % sizes[1]],
                    grads_out[which].at[mask - 1],
                    part_send.at[which, mask],
                    part_recv.at[which, mask],
                    mask,
                )
            )
    own = []
    for which in range(count):
        own.append(
            pltpu.make_async_copy(
                rows[which].at[cube.dp], rows_out[which].at[cube.dp], local_sems.at[which]
            )
        )
        own[-1].start()
    for copy in pending:
        copy.wait_recv()
    for copy in own:
        copy.wait()
    for copy in pending:
        copy.wait_send()


def swap_rows(sizes, rows, grads, collective_id, name):
    count, parts = (len(rows), len(grads))
    peers = max(sizes[1] - 1, 1)
    out_shape = [jax.ShapeDtypeStruct(part.shape, part.dtype) for part in rows]
    out_shape += [
        jax.ShapeDtypeStruct((peers,) + part.shape[1:], part.dtype) for part in grads
    ]
    dma = pltpu.SemaphoreType.DMA
    return pl.pallas_call(
        lambda *refs: swap_kernel(sizes, count, parts, *refs),
        out_shape=tuple(out_shape),
        in_specs=[pl.BlockSpec(memory_space=pltpu.VMEM)] * (count + parts),
        out_specs=(pl.BlockSpec(memory_space=pl.ANY),) * (count + parts),
        scratch_shapes=[
            dma((count,)),
            dma((count, sizes[0])),
            dma((count, sizes[0])),
            dma((max(parts, 1), sizes[1])),
            dma((max(parts, 1), sizes[1])),
        ],
        compiler_params=pltpu.CompilerParams(
            collective_id=collective_id,
            has_side_effects=True,
            vmem_limit_bytes=24 * 1024 * 1024,
        ),
        name=name,
    )(*rows, *grads)


def scatter_kernel(sizes, count, *refs):
    sources, outs = (refs[:count], refs[count : 2 * count])
    slots, held = (refs[2 * count : 3 * count], refs[3 * count : 4 * count])
    send_sems, recv_sems = refs[4 * count :]
    cube = Cube(sizes)
    cube.greet([1 << bit for bit in range(cube.bits)])
    orders = [bit_order(sizes, letters)[::-1] for letters in SCATTER_ORDERS]
    copies = [{} for _ in sources]
    arrived = [set() for _ in sources]
    places = [{} for _ in sources]

    def total(which, mask, stage):
        value = sources[which][cube.block(mask)].astype(jnp.float32)
        for earlier in orders[which][:stage]:
            label = mask | (1 << earlier)
            copies[which][label].wait_recv()
            value = value + slots[which][label].astype(jnp.float32)
        return value

    for which, stage, mask in scatter_plan(
        sizes, orders, [volume_of(ref.shape) / 23e3 for ref in outs], SCATTER_LAG
    ):
        if stage == 0:
            leaving = sources[which].at[cube.block(mask)]
        else:
            slot = places[which].setdefault(mask, len(places[which]))
            held[which][slot] = total(which, mask, stage).astype(jnp.bfloat16)
            leaving = held[which].at[slot]
        copies[which][mask] = cube.send(
            leaving,
            slots[which].at[mask],
            send_sems.at[which, mask],
            recv_sems.at[which, mask],
            1 << orders[which][stage],
        )
    for which in range(count):
        outs[which][...] = total(which, 0, len(orders[which]))
    for made in copies:
        for copy in made.values():
            copy.wait_send()


def scatter_rows(sizes, packed):
    blocks = sizes[0] * sizes[1]
    count = len(packed)
    shapes = [part.shape[1:] for part in packed]
    dma = pltpu.SemaphoreType.DMA
    return pl.pallas_call(
        lambda *refs: scatter_kernel(sizes, count, *refs),
        out_shape=tuple(jax.ShapeDtypeStruct(shape, jnp.float32) for shape in shapes),
        in_specs=[pl.BlockSpec(memory_space=pltpu.VMEM)] * count,
        out_specs=(pl.BlockSpec(memory_space=pltpu.VMEM),) * count,
        scratch_shapes=[pltpu.VMEM((blocks,) + shape, jnp.bfloat16) for shape in shapes]
        + [pltpu.VMEM((blocks // 2,) + shape, jnp.bfloat16) for shape in shapes]
        + [dma((count, blocks)), dma((count, blocks))],
        compiler_params=pltpu.CompilerParams(
            collective_id=3, has_side_effects=True, vmem_limit_bytes=48 * 1024 * 1024
        ),
        name="scatter_rows",
    )(*packed)


def lanes_of(shape):
    return lax.broadcasted_iota(jnp.int32, shape, 1)


def rows_of(shape):
    return lax.broadcasted_iota(jnp.int32, shape, 0)


def dot(left, right):
    return jnp.dot(left, right, preferred_element_type=jnp.float32)


def dot_nt(left, right):
    return lax.dot_general(
        left, right, (((1,), (1,)), ((), ())), preferred_element_type=jnp.float32
    )


def dot_tn(left, right):
    return lax.dot_general(
        left, right, (((0,), (0,)), ((), ())), preferred_element_type=jnp.float32
    )


def half(values):
    return values.astype(jnp.bfloat16)


def wide(values):
    return values.astype(jnp.float32)


def masks_of(doc_ref):
    count = doc_ref.shape[1]
    doc_row = jnp.broadcast_to(doc_ref[...].astype(jnp.float32), (count, count))
    doc_col = doc_row.T
    same = doc_row == doc_col
    row, lane = (rows_of((count, count)), lanes_of((count, count)))
    position = jnp.sum(jnp.where(same & (lane < row), 1.0, 0.0), axis=1, keepdims=True)
    allowed = same & (lane <= row)
    live = jnp.where(doc_col[:, :1] < count, 1.0, 0.0)
    return (position, allowed, live)


def slots_in_kernel(ids_ref, live, experts):
    count = ids_ref.shape[0]
    lane = lanes_of((count, 128))
    ids = ids_ref[...]
    chosen = jnp.zeros((count, 128), jnp.float32)
    for top in range(ids.shape[1]):
        chosen = chosen + jnp.where(ids[:, top : top + 1] == lane, 1.0, 0.0)
    member = chosen * live
    lower = jnp.where(lanes_of((count, count)) < rows_of((count, count)), 1.0, 0.0)
    rank = dot(half(lower), half(member))
    kept = jnp.where(rank < CAP, member, 0.0)
    place = jnp.where(kept > 0.0, rank, -1.0).T[:experts]
    slot = lax.broadcasted_iota(jnp.int32, (experts, CAP, count), 1).astype(jnp.float32)
    dispatch = jnp.where(place[:, None, :] == slot, 1.0, 0.0)
    return (chosen, dispatch)


def rope_in_kernel(position):
    lane = lanes_of((position.shape[0], 128))
    half_dim = HEAD_DIM // 2
    step = (lane % half_dim).astype(jnp.float32)
    freqs = jnp.exp(-jnp.log(10000.0) * (2.0 * step / HEAD_DIM))
    angle = position * freqs
    first = lane % HEAD_DIM < half_dim
    sinusoid = jnp.sin(angle)
    return (jnp.cos(angle), jnp.where(first, -sinusoid, sinusoid), first)


def swap_halves(values, first):
    width = values.shape[1]
    half_dim = HEAD_DIM // 2
    return jnp.where(
        first, pltpu.roll(values, width - half_dim, 1), pltpu.roll(values, half_dim, 1)
    )


def doubled(tile, odd):
    front = lanes_of(tile.shape) < HEAD_DIM
    rolled = pltpu.roll(tile, HEAD_DIM, 1)
    return half(jnp.where(front, rolled, tile) if odd else jnp.where(front, tile, rolled))


def stacked(tile):
    front = lanes_of(tile.shape) < HEAD_DIM
    return half(
        jnp.concatenate([jnp.where(front, tile, 0.0), jnp.where(front, 0.0, tile)], axis=0)
    )


def unstacked(pair):
    count = pair.shape[0] // 2
    front = lanes_of((count, pair.shape[1])) < HEAD_DIM
    return jnp.where(front, pair[:count], pair[count:])


def tile_of(at):
    return slice(128 * at, 128 * at + 128)


def small_rows(small_ref, experts):
    pick = jnp.where(lanes_of((8, 128)) == rows_of((8, 128)) + experts, 1.0, 0.0)
    picked = dot_nt(half(pick), small_ref[...])
    return (picked[0:1], picked[1:2])


def norm_in_kernel(values):
    scale_row = lax.rsqrt(jnp.mean(values * values, axis=1, keepdims=True) + norm_eps)
    return (values * scale_row, scale_row)


def forward_kernel(
    experts,
    hidden_ref,
    doc_ref,
    ids_ref,
    query_ref,
    key_ref,
    value_ref,
    output_ref,
    small_ref,
    rows_out,
    mid_out,
    q_out,
    k_out,
    v_out,
    p_out,
    o_out,
    routed_out,
    gates_out,
):
    scale = HEAD_DIM ** (-0.5)
    position, allowed, live = masks_of(doc_ref)
    chosen, dispatch = slots_in_kernel(ids_ref, live, experts)
    cosine, sinusoid, first = rope_in_kernel(position)
    gain_one, gain_two = small_rows(small_ref, experts)
    resid = wide(hidden_ref[...])
    normed, _ = norm_in_kernel(resid)
    h1 = half(normed * gain_one)
    key_raw = dot(h1, key_ref[...])
    for at in range(key_raw.shape[1] // 128):
        part = key_raw[:, tile_of(at)]
        k_out[:, tile_of(at)] = half(part * cosine + swap_halves(part, first) * sinusoid)
    v_out[...] = half(dot(h1, value_ref[...]))
    query_raw = dot(h1, query_ref[...])
    both = jnp.concatenate([allowed, allowed], axis=0)
    for head in range(KV_HEADS):
        part = query_raw[:, tile_of(head)]
        turned = half(part * cosine + swap_halves(part, first) * sinusoid)
        q_out[:, tile_of(head)] = turned
        keys = doubled(wide(k_out[:, tile_of(head // 2)]), head % 2)
        values = doubled(wide(v_out[:, tile_of(head // 2)]), head % 2)
        scores = dot_nt(stacked(wide(turned)), keys) * scale
        raised = jnp.where(both, jnp.exp(scores), 0.0)
        total = jnp.log(jnp.sum(raised, axis=1, keepdims=True))
        probs = jnp.where(both, jnp.exp(scores - total), 0.0)
        p_out[head] = probs
        o_out[:, tile_of(head)] = half(unstacked(dot(half(probs), values)) * live)
    mid = resid + dot(o_out[...], output_ref[...])
    mid_out[...] = mid
    normed_two, _ = norm_in_kernel(mid)
    h2 = half(normed_two * gain_two)
    routed_out[...] = h2
    logits = dot(h2, small_ref[...])
    raised = jnp.where(chosen > 0.0, jnp.exp(logits), 0.0)
    gates = raised / jnp.sum(raised, axis=1, keepdims=True)
    gates_t = gates.T[:experts]
    gates_out[...] = gates_t
    slots = experts * CAP
    one_hot = half(dispatch.reshape(slots, -1))
    slot_gate = jnp.sum(
        (dispatch * gates_t[:, None, :]).reshape(slots, -1), axis=1, keepdims=True
    )
    high = wide(half(slot_gate))
    middle = wide(half(slot_gate - high))
    low = slot_gate - high - middle
    lane = lanes_of((slots, 128))
    packed = jnp.where(
        lane == 0, high, jnp.where(lane == 1, middle, jnp.where(lane == 2, low, 0.0))
    )
    width = h2.shape[1]
    sent = dot(one_hot, h2)
    for e in range(experts):
        rows_out[e, :, :width] = half(sent[e * CAP : (e + 1) * CAP])
        rows_out[e, :, width:] = half(packed[e * CAP : (e + 1) * CAP])


def expert_kernel(rows_ref, grads_ref, gate_ref, up_ref, down_ref, out_ref, back_ref, *grads_out):
    width = grads_ref.shape[1]
    rows = rows_ref[:, :width]
    slot_gate = jnp.sum(wide(rows_ref[:, width:]), axis=1, keepdims=True)
    grad_rows = half(slot_gate * wide(grads_ref[...]))
    gate_pre = dot(rows, gate_ref[...])
    up_pre = dot(rows, up_ref[...])
    sigmoid_gate = 1.0 / (1.0 + jnp.exp(-gate_pre))
    act = half(gate_pre * sigmoid_gate * up_pre)
    out_ref[...] = half(dot(act, down_ref[...]))
    grad_act = dot_nt(grad_rows, down_ref[...])
    grad_up = half(grad_act * gate_pre * sigmoid_gate)
    grad_gate = half(grad_act * up_pre * sigmoid_gate * (1.0 + gate_pre * (1.0 - sigmoid_gate)))
    back_ref[...] = half(dot_nt(grad_gate, gate_ref[...]) + dot_nt(grad_up, up_ref[...]))
    made = (dot_tn(rows, grad_gate), dot_tn(rows, grad_up), dot_tn(act, grad_rows))
    for which, value in enumerate(made):
        grads_out[which][...] = value
        grads_out[which + 3][...] = half(value)


def backward_kernel(
    experts,
    hidden_ref,
    doc_ref,
    ids_ref,
    grad_ref,
    query_ref,
    key_ref,
    value_ref,
    output_ref,
    small_ref,
    mid_ref,
    q_ref,
    k_ref,
    v_ref,
    p_ref,
    o_ref,
    routed_ref,
    gates_ref,
    back_ref,
    slots_ref,
    layer_out,
    input_out,
    query_out,
    key_out,
    value_out,
    output_out,
    small_out,
    dq_ref,
    dk_ref,
    dv_ref,
    ready=lambda which: None,
):
    scale = HEAD_DIM ** (-0.5)
    position, _, live = masks_of(doc_ref)
    _, dispatch = slots_in_kernel(ids_ref, live, experts)
    cosine, sinusoid, first = rope_in_kernel(position)
    gain_one, gain_two = small_rows(small_ref, experts)
    slots = experts * CAP
    count = doc_ref.shape[1]
    gates = gates_ref[...]
    combine = (dispatch * gates[:, None, :]).reshape(slots, count).T
    combine_high = half(combine)
    combine_low = half(combine - wide(combine_high))
    flat = dispatch.reshape(slots, count)
    flat_t = half(flat.T)
    mid = mid_ref[...]
    out_rows = back_ref[...]
    layer_out[...] = half(mid + (dot(combine_high, out_rows) + dot(combine_low, out_rows)))
    row_dots = dot_nt(out_rows, grad_ref[...])
    grad_gates = jnp.sum((flat * row_dots).reshape(experts, CAP, count), axis=1)
    grad_logits = gates * (grad_gates - jnp.sum(gates * grad_gates, axis=0, keepdims=True))
    logit_rows = jnp.concatenate(
        [grad_logits, jnp.zeros((128 - experts, count), jnp.float32)], axis=0
    )
    logits_t = half(logit_rows.T)
    grad_router = dot(half(logit_rows), routed_ref[...])
    grad_routed = dot(flat_t, slots_ref[...]) + dot_nt(logits_t, small_ref[...])
    normed_two, scale_two = norm_in_kernel(mid)
    scaled = grad_routed * gain_two
    inner = jnp.mean(scaled * normed_two, axis=1, keepdims=True)
    grad_gain_two = jnp.sum(grad_routed * normed_two, axis=0, keepdims=True)
    grad_mid = wide(grad_ref[...]) + scale_two * (scaled - normed_two * inner)
    grad_mid_b = half(grad_mid)
    output_out[...] = half(dot_tn(o_ref[...], grad_mid_b))
    ready(3)
    grad_mixed = half(dot_nt(grad_mid_b, output_ref[...]) * live)
    front = lanes_of((count, 128)) < HEAD_DIM
    pair = {}
    for head in range(KV_HEADS):
        keys = doubled(wide(k_ref[:, tile_of(head // 2)]), head % 2)
        values = doubled(wide(v_ref[:, tile_of(head // 2)]), head % 2)
        queries = stacked(wide(q_ref[:, tile_of(head)]))
        mixed = stacked(wide(grad_mixed[:, tile_of(head)]))
        probs = p_ref[head]
        grad_probs = dot_nt(mixed, values)
        delta = jnp.sum(probs * grad_probs, axis=1, keepdims=True)
        grad_scores = half(probs * (grad_probs - delta) * scale)
        part = unstacked(dot(grad_scores, keys))
        dq_ref[:, tile_of(head)] = half(part * cosine - swap_halves(part, first) * sinusoid)
        grad_key = dot_tn(grad_scores, queries)
        grad_value = dot_tn(half(probs), mixed)
        pair[head % 2] = (
            grad_key + pltpu.roll(grad_key, HEAD_DIM, 1),
            grad_value + pltpu.roll(grad_value, HEAD_DIM, 1),
        )
        if head % 2:
            part = jnp.where(front, pair[0][0], pair[1][0])
            dk_ref[:, tile_of(head // 2)] = half(
                part * cosine - swap_halves(part, first) * sinusoid
            )
            dv_ref[:, tile_of(head // 2)] = half(jnp.where(front, pair[0][1], pair[1][1]))
    resid = wide(hidden_ref[...])
    normed_one, scale_one = norm_in_kernel(resid)
    h1 = half(normed_one * gain_one)
    query_out[...] = half(dot_tn(h1, dq_ref[...]))
    ready(0)
    key_out[...] = half(dot_tn(h1, dk_ref[...]))
    ready(1)
    value_out[...] = half(dot_tn(h1, dv_ref[...]))
    ready(2)
    grad_normed = dot_nt(dq_ref[...], query_ref[...])
    grad_normed = grad_normed + dot_nt(dk_ref[...], key_ref[...])
    grad_normed = grad_normed + dot_nt(dv_ref[...], value_ref[...])
    scaled = grad_normed * gain_one
    inner = jnp.mean(scaled * normed_one, axis=1, keepdims=True)
    grad_gain_one = jnp.sum(grad_normed * normed_one, axis=0, keepdims=True)
    input_out[...] = half(grad_mid + scale_one * (scaled - normed_one * inner))
    row = rows_of(grad_router.shape)
    small = jnp.where(
        row < experts,
        grad_router,
        jnp.where(row == experts, grad_gain_one, jnp.where(row == experts + 1, grad_gain_two, 0.0)),
    )
    small_out[...] = half(small.T)
    ready(4)


def plain_call(kernel, name, outs, scratch, *args):
    return pl.pallas_call(
        kernel,
        out_shape=tuple(jax.ShapeDtypeStruct(shape, dtype) for shape, dtype in outs),
        in_specs=[pl.BlockSpec(memory_space=pltpu.VMEM)] * len(args),
        out_specs=(pl.BlockSpec(memory_space=pltpu.VMEM),) * len(outs),
        scratch_shapes=[pltpu.VMEM(shape, dtype) for shape, dtype in scratch],
        compiler_params=pltpu.CompilerParams(vmem_limit_bytes=60 * 1024 * 1024),
        name=name,
    )(*args)


class Flat:
    def __init__(self, ref):
        self.ref = ref

    def __getitem__(self, at):
        return self.ref[...].reshape(-1, self.ref.shape[-1])

    def __setitem__(self, at, value):
        self.ref[...] = value.reshape(self.ref.shape)


class Slots:
    def __init__(self, ref):
        self.ref = ref

    def __getitem__(self, at):
        return half(wide(self.ref[...]).reshape(-1, self.ref.shape[-1]))


def step_kernel(sizes, experts, *refs):
    hidden, doc, ids, grad = refs[:4]
    shards, router, gains, weights = (list(refs[4:8]), refs[8], refs[9:11], refs[11:14])
    layer_out, input_out = refs[14:16]
    outs, own_out, other_out = (refs[16:21], refs[21:24], refs[24:27])
    full, wide_refs = (refs[27:32], refs[32:35])
    small_src, pulled, pulled_in, rows_src, rows_in = refs[35:40]
    y_src, x_src, y_in, x_in = refs[40:44]
    saved = refs[44:52]
    sums, sums_half = (refs[52:55], refs[55:58])
    grads, slots, held = (refs[58:63], refs[63:68], refs[68:73])
    turned = refs[73:76]
    (
        local_sems,
        send_sems,
        recv_sems,
        wide_send,
        wide_recv,
        row_send,
        row_recv,
        part_send,
        part_recv,
        back_send,
        back_recv,
    ) = refs[76:]
    cube = Cube(sizes)
    width = hidden.shape[1]
    singles = [1 << bit for bit in range(cube.bits)]
    cube.greet(sorted(set(singles + cube.dp_masks() + cube.fsdp_masks())))
    local = []

    def keep(source, target):
        local.append(pltpu.make_async_copy(source, target, local_sems.at[len(local)]))
        local[-1].start()
        return local[-1]

    depth = router.shape[0]
    eye = lanes_of((depth, depth)) == rows_of((depth, depth))
    lane = lanes_of((depth, 128))
    pick = jnp.where(lanes_of((experts, 128)) == rows_of((experts, 128)), 1.0, 0.0)
    small = dot(router[...], half(pick))
    for at, gain in enumerate(gains):
        column = jnp.sum(jnp.where(eye, wide(gain[...]), 0.0), axis=1, keepdims=True)
        small = jnp.where(lane == experts + at, column, small)
    small_src[...] = half(small)
    shards.append(small_src)

    leaving = []
    fills = []
    letters = dimension_bits(sizes)
    peers = sorted(cube.dp_masks())
    for piece in range(EXPERT_PIECES):
        for which, source in enumerate(weights):
            for mask in cube.fsdp_masks():
                volume = volume_of(source.shape) / EXPERT_PIECES
                fills.append(("x", volume, ("expert", which, mask, piece)))
    for peer in peers:
        link = [letter for letter in "zyc" if any(peer >> bit & 1 for bit in letters[letter])][0]
        fills.append((link, volume_of(pulled.shape[1:]), ("row", peer)))

    def rows_to(peer, source, target, which):
        part = peer >> cube.fsdp_bits
        copy = cube.send(
            source.at[cube.block(peer) // sizes[1]],
            target.at[cube.dp],
            row_send.at[which, part],
            row_recv.at[which, part],
            peer,
        )
        leaving.append(copy)
        return copy

    def fill(kind, *rest):
        if kind == "row":
            return rows_to(rest[0], pulled, pulled_in, 0)
        which, mask, piece = rest
        share = weights[which].shape[1] // EXPERT_PIECES
        place = pl.ds(piece * share, share)
        at = mask * EXPERT_PIECES + piece
        leaving.append(
            cube.send(
                weights[which].at[0, place],
                wide_refs[which].at[cube.fsdp, place],
                wide_send.at[which, at],
                wide_recv.at[which, at],
                mask,
            )
        )
        return leaving[-1]

    def prepare():
        for which, source in enumerate(shards):
            keep(source, full[which].at[cube.me])
        for which, source in enumerate(weights):
            keep(source.at[0], wide_refs[which].at[cube.fsdp])
        _, _, live = masks_of(doc)
        _, dispatch = slots_in_kernel(ids, live, experts)
        moved = dot(half(dispatch.reshape(experts * CAP, -1)), grad[...])
        for e in range(experts):
            pulled[e] = half(moved[e * CAP : (e + 1) * CAP])

    orders = [bit_order(sizes, order) for order in STEP_ORDERS]
    unit = 46e3 / 2
    plan = gather_plan(
        sizes,
        orders,
        [volume_of(ref.shape[1:]) / unit for ref in full],
        [(link, volume / unit) for link, volume, _ in fills],
        GATHER_LAG,
        GATHER_LEAD,
    )
    made = [{} for _ in shards]
    arrived = [{0} for _ in shards]
    filled = []
    started = False
    for which, mask, bit in plan:
        if not started and (fills[mask][2][0] == "row" if which is None else mask):
            started = True
            prepare()
        if which is None:
            filled.append(fill(*fills[mask][2]))
            continue
        if mask not in arrived[which]:
            made[which][mask].wait_recv()
            arrived[which].add(mask)
        label = mask | (1 << bit)
        target = full[which].at[cube.block(mask)]
        made[which][label] = cube.send(
            target if mask else shards[which],
            target,
            send_sems.at[0, which, label],
            recv_sems.at[0, which, label],
            1 << bit,
        )
        leaving.append(made[which][label])
    for which, part in enumerate(made):
        for label, copy in part.items():
            if label not in arrived[which]:
                copy.wait_recv()
    for copy in local:
        copy.wait()
    dense = [Flat(ref) for ref in full]
    forward_kernel(experts, hidden, doc, ids, *dense, rows_src, *saved)
    coming = [rows_to(peer, rows_src, rows_in, 1) for peer in peers]
    mine = [keep(pulled.at[cube.dp], pulled_in.at[cube.dp])]
    mine.append(keep(rows_src.at[cube.dp], rows_in.at[cube.dp]))
    for copy in filled + coming:
        copy.wait_recv()
    for copy in mine:
        copy.wait()

    packed = wide(rows_in[...]).reshape(experts * CAP, -1)
    rows = half(packed[:, :width])
    slot_gate = jnp.sum(packed[:, width:], axis=1, keepdims=True)
    grad_rows = half(slot_gate * wide(pulled_in[...]).reshape(experts * CAP, -1))
    w_gate, w_up, w_down = [Flat(ref)[...] for ref in wide_refs]
    gate_pre = dot(rows, w_gate)
    up_pre = dot(rows, w_up)
    sigmoid_gate = 1.0 / (1.0 + jnp.exp(-gate_pre))
    act = half(gate_pre * sigmoid_gate * up_pre)
    grad_act = dot_nt(grad_rows, w_down)
    grad_up = half(grad_act * gate_pre * sigmoid_gate)
    grad_gate = half(grad_act * up_pre * sigmoid_gate * (1.0 + gate_pre * (1.0 - sigmoid_gate)))

    def give(values, source, target, which):
        for e in range(experts):
            source[e] = half(values[e * CAP : (e + 1) * CAP])
        copies = [rows_to(peer, source, target, which) for peer in peers]
        return (copies, keep(source.at[cube.dp], target.at[cube.dp]))

    coming, kept = give(dot(act, w_down), y_src, y_in, 2)
    more, kept_more = give(dot_nt(grad_gate, w_gate) + dot_nt(grad_up, w_up), x_src, x_in, 3)
    exchanged = []
    pairs = ((rows, grad_gate), (rows, grad_up), (act, grad_rows))
    for which, (left, right) in enumerate(pairs):
        value = dot_tn(left, right).reshape(sums[which].shape)
        sums[which][...] = value
        sums_half[which][...] = half(value)
        for mask in cube.fsdp_masks():
            exchanged.append(
                cube.send(
                    sums_half[which].at[cube.block(mask) % sizes[1]],
                    other_out[which].at[mask - 1],
                    part_send.at[which, mask],
                    part_recv.at[which, mask],
                    mask,
                )
            )
    last = [keep(sums[which].at[cube.fsdp], own_out[which]) for which in range(3)]
    for copy in coming + more:
        copy.wait_recv()
    kept.wait()
    kept_more.wait()

    back_orders = [bit_order(sizes, order)[::-1] for order in SCATTER_ORDERS]
    back = [{} for _ in grads]
    seen = [{} for _ in grads]

    def total(which, mask, stage):
        value = wide(grads[which][cube.block(mask)])
        for earlier in back_orders[which][:stage]:
            label = mask | (1 << earlier)
            back[which][label].wait_recv()
            value = value + wide(slots[which][label])
        return value

    def pass_on(which, stage, mask):
        if stage == 0:
            going = grads[which].at[cube.block(mask)]
        else:
            slot = seen[which].setdefault(mask, len(seen[which]))
            held[which][slot] = half(total(which, mask, stage))
            going = held[which].at[slot]
        back[which][mask] = cube.send(
            going,
            slots[which].at[mask],
            back_send.at[which, mask],
            back_recv.at[which, mask],
            1 << back_orders[which][stage],
        )
        leaving.append(back[which][mask])

    steps = scatter_plan(
        sizes, back_orders, [volume_of(ref.shape) / 23e3 for ref in outs], SCATTER_LAG
    )

    def ready(which):
        for step in steps:
            if step[0] == which and step[1] == 0:
                pass_on(*step)

    backward_kernel(
        experts,
        hidden,
        doc,
        ids,
        grad,
        *dense,
        *saved,
        Slots(y_in),
        Slots(x_in),
        layer_out,
        input_out,
        *[Flat(ref) for ref in grads],
        *turned,
        ready=ready,
    )
    for step in steps:
        if step[1]:
            pass_on(*step)
    for which, out in enumerate(outs):
        out[...] = total(which, 0, len(back_orders[which]))
    for copy in exchanged:
        copy.wait_recv()
        copy.wait_send()
    for copy in last:
        copy.wait()
    for copy in leaving:
        copy.wait_send()


STEP_ORDERS = ("zyxc", "xyzc", "zyxc", "zxyc", "zxyc")


def step_call(sizes, experts, streams, tokens, router, gains, weights):
    hidden, doc, ids, grad = tokens
    rows, width = hidden.shape
    blocks = sizes[0] * sizes[1]
    bf16, f32 = (jnp.bfloat16, jnp.float32)
    shapes = [part.shape for part in streams] + [(router.shape[0], 128)]
    query_width, key_width = (streams[0].shape[1], streams[1].shape[1])
    shares = [part.shape[1:] for part in weights]
    spread = [(sizes[1],) + share for share in shares]
    slot_rows = (experts, CAP, width)
    tail = (experts, CAP, width + 128)
    others = max(sizes[1] - 1, 1)
    vmem, any_space = (pl.BlockSpec(memory_space=pltpu.VMEM), pl.BlockSpec(memory_space=pl.ANY))
    scratch = [((blocks,) + shape, bf16) for shape in shapes]
    scratch += [(shape, bf16) for shape in spread]
    scratch += [(shapes[-1], bf16), (slot_rows, bf16), (slot_rows, bf16), (tail, bf16), (tail, bf16)]
    scratch += [(slot_rows, bf16)] * 4
    scratch += [
        ((rows, width), f32),
        ((rows, query_width), bf16),
        ((rows, key_width), bf16),
        ((rows, key_width), bf16),
        ((KV_HEADS, 2 * rows, rows), f32),
        ((rows, query_width), bf16),
        ((rows, width), bf16),
        ((experts, rows), f32),
    ]
    scratch += [(shape, f32) for shape in spread] + [(shape, bf16) for shape in spread]
    scratch += [((blocks,) + shape, bf16) for shape in shapes] * 2
    scratch += [((blocks // 2,) + shape, bf16) for shape in shapes]
    scratch += [((rows, query_width), bf16), ((rows, key_width), bf16), ((rows, key_width), bf16)]
    dma = pltpu.SemaphoreType.DMA
    sems = [
        dma((16,)),
        dma((1, 5, blocks)),
        dma((1, 5, blocks)),
        dma((3, sizes[1] * EXPERT_PIECES)),
        dma((3, sizes[1] * EXPERT_PIECES)),
        dma((4, sizes[0])),
        dma((4, sizes[0])),
        dma((3, sizes[1])),
        dma((3, sizes[1])),
        dma((5, blocks)),
        dma((5, blocks)),
    ]
    outs = [((rows, width), bf16)] * 2 + [(shape, f32) for shape in shapes]
    outs += [(share, f32) for share in shares] + [((others,) + share, bf16) for share in shares]
    return pl.pallas_call(
        lambda *refs: step_kernel(sizes, experts, *refs),
        out_shape=tuple(jax.ShapeDtypeStruct(shape, dtype) for shape, dtype in outs),
        in_specs=[vmem] * 4 + [any_space] * 4 + [vmem] * 3 + [any_space] * 3,
        out_specs=(vmem,) * 7 + (any_space,) * 6,
        scratch_shapes=[pltpu.VMEM(shape, dtype) for shape, dtype in scratch] + sems,
        compiler_params=pltpu.CompilerParams(
            collective_id=4, has_side_effects=True, vmem_limit_bytes=60 * 1024 * 1024
        ),
        name="step",
    )(hidden, doc, ids, grad, *streams, router, *gains, *weights)


def shards(
    sizes,
    hidden_in,
    doc_id,
    expert_ids,
    out_grad,
    attn_gain,
    query_weight,
    key_weight,
    value_weight,
    output_weight,
    ffn_gain,
    router_weight,
    expert_gate,
    expert_up,
    expert_down,
):
    rows, width = hidden_in.shape
    experts = router_weight.shape[1]
    blocks = sizes[0] * sizes[1]
    query_width, key_width = (query_weight.shape[1], key_weight.shape[1])
    if query_weight.shape[0] % 16 == 0:
        step = step_call(
            sizes,
            experts,
            (query_weight, key_weight, value_weight, output_weight),
            (hidden_in, doc_id.reshape(1, rows), expert_ids, out_grad),
            router_weight,
            (attn_gain.reshape(1, -1), ffn_gain.reshape(1, -1)),
            (expert_gate, expert_up, expert_down),
        )
        expert_grads = [
            mine[None] + jnp.sum(other.astype(jnp.float32), axis=0, keepdims=True)
            for mine, other in zip(step[7:10], step[10:13])
        ]
        own_small = step[6]
        return (
            step[0],
            step[1],
            own_small[:, experts],
            *step[2:6],
            own_small[:, experts + 1],
            own_small[:, :experts],
            *expert_grads,
        )
    hidden_units = expert_gate.shape[2]
    small = jnp.concatenate([router_weight, attn_gain[:, None], ffn_gain[:, None]], axis=1)
    small = jnp.pad(small, ((0, 0), (0, 128 - small.shape[1])))
    doc_row = doc_id.reshape(1, rows)
    slots = experts * CAP
    bf16, f32 = (jnp.bfloat16, jnp.float32)
    live_rows = (doc_id < rows).astype(f32)
    dispatch, _, _, _ = slots_of(expert_ids, live_rows, experts)
    pulled_b = jnp.einsum(
        "ecr,rd->ecd", dispatch.astype(bf16), out_grad, preferred_element_type=f32
    ).astype(bf16)
    gathered = front_gather(
        sizes,
        (query_weight, key_weight, value_weight, output_weight, small),
        (expert_gate[0], expert_up[0], expert_down[0]),
        pulled_b,
    )
    dense = [part.reshape(-1, part.shape[2]) for part in gathered[:5]]
    wide_experts = [part.reshape(-1, part.shape[2]) for part in gathered[5:8]]
    saved = plain_call(
        functools.partial(forward_kernel, experts),
        "forward",
        [
            ((experts, CAP, width + 128), bf16),
            ((rows, width), f32),
            ((rows, query_width), bf16),
            ((rows, key_width), bf16),
            ((rows, key_width), bf16),
            ((KV_HEADS, 2 * rows, rows), f32),
            ((rows, query_width), bf16),
            ((rows, width), bf16),
            ((experts, rows), f32),
        ],
        [],
        hidden_in,
        doc_row,
        expert_ids,
        *dense,
    )
    (recv,) = swap_rows(sizes, (saved[0],), (), 1, "swap_out")
    made = plain_call(
        expert_kernel,
        "experts",
        [((slots, width), bf16)] * 2
        + [((width, hidden_units), f32)] * 2
        + [((hidden_units, width), f32)]
        + [((width, hidden_units), bf16)] * 2
        + [((hidden_units, width), bf16)],
        [],
        recv.reshape(slots, -1),
        gathered[8].reshape(slots, width),
        *wide_experts,
    )
    swapped = swap_rows(
        sizes,
        [part.reshape(experts, CAP, width) for part in made[:2]],
        [part.reshape((sizes[1], -1) + part.shape[1:]) for part in made[5:]],
        2,
        "swap_back",
    )
    own = lax.axis_index("fsdp")
    expert_grads = [
        lax.dynamic_index_in_dim(
            mine.reshape((sizes[1], -1) + mine.shape[1:]), own, axis=0, keepdims=True
        )
        + jnp.sum(other.astype(f32), axis=0, keepdims=True)
        for mine, other in zip(made[2:5], swapped[2:])
    ]
    results = plain_call(
        functools.partial(backward_kernel, experts),
        "backward",
        [
            ((rows, width), bf16),
            ((rows, width), bf16),
            ((width, query_width), bf16),
            ((width, key_width), bf16),
            ((width, key_width), bf16),
            ((query_width, width), bf16),
            ((width, 128), bf16),
        ],
        [((rows, query_width), bf16), ((rows, key_width), bf16), ((rows, key_width), bf16)],
        hidden_in,
        doc_row,
        expert_ids,
        out_grad,
        *dense,
        *saved[1:],
        swapped[0].reshape(slots, width),
        swapped[1].reshape(slots, width),
    )
    own_query, own_key, own_value, own_output, own_small = scatter_rows(
        sizes, [part.reshape(blocks, -1, part.shape[1]) for part in results[2:]]
    )
    return (
        results[0],
        results[1],
        own_small[:, experts],
        own_query,
        own_key,
        own_value,
        own_output,
        own_small[:, experts + 1],
        own_small[:, :experts],
        expert_grads[0],
        expert_grads[1],
        expert_grads[2],
    )


def solution(mesh):
    in_specs = (
        P(("dp", "fsdp"), None),
        P(("dp", "fsdp")),
        P(("dp", "fsdp"), None),
        P(("dp", "fsdp"), None),
        P(("dp", "fsdp")),
        P(("dp", "fsdp"), None),
        P(("dp", "fsdp"), None),
        P(("dp", "fsdp"), None),
        P(("dp", "fsdp"), None),
        P(("dp", "fsdp")),
        P(("dp", "fsdp"), None),
        P("dp", "fsdp", None),
        P("dp", "fsdp", None),
        P("dp", "fsdp", None),
    )
    out_specs = (
        P(("dp", "fsdp"), None),
        P(("dp", "fsdp"), None),
        P(("dp", "fsdp")),
        P(("dp", "fsdp"), None),
        P(("dp", "fsdp"), None),
        P(("dp", "fsdp"), None),
        P(("dp", "fsdp"), None),
        P(("dp", "fsdp")),
        P(("dp", "fsdp"), None),
        P("dp", "fsdp", None),
        P("dp", "fsdp", None),
        P("dp", "fsdp", None),
    )
    sizes = (mesh.shape["dp"], mesh.shape["fsdp"])
    body = functools.partial(shards, sizes)
    return jax.shard_map(body, mesh=mesh, in_specs=in_specs, out_specs=out_specs, check_vma=False)
```
